32 devices in a mesh: grp: 4 (over x, core), mem: 8 (over z, y).
Axes of the slice: x: 2, y: 2, z: 4, core: 2. Of those that a mesh axis runs over, the one named last changes fastest.
Arguments:
- features: bfloat16 [32768, 4096], P(('grp', 'mem')), may hold values from -0.09375 to 0.09375
- re_features: bfloat16 [32768, 256], P(('grp', 'mem')), may hold values from -6 to 6
- member_id: int32 [32768], P(('grp', 'mem')), may hold values from 0 to 255, as said below
- slot: int32 [32768], P(('grp', 'mem')), may hold values from 0 to 2047, as said below
- labels: int32 [32768], P(('grp', 'mem')), may hold values 0 or 1
- offsets: float32 [32768], P(('grp', 'mem')), may hold values from -6 to 6
- feature_scale: float32 [4096], replicated, may hold values from 0.3 to 3
- w_start: float32 [4096], replicated, may hold values from -4 to 4
Outputs:
- fixed_weights: float32 [4096], replicated
- member_coef: float32 [256, 256], P(('grp', 'mem'))
- row_offsets: float32 [32768], P(('grp', 'mem'))
The draws below stay inside these ranges and needn't reach their ends.
Inputs may be any that keep to these rules, and one draw needn't show every extreme that they name: A row of device k (devices counted along grp, then mem) belongs to group k // 8: member_id // 64 is that group, and (member_id mod 64) // 8 equals slot // 256. Rows per member are uneven. Within one device's rows the slots are distinct; slot // 256 is the mem index that owns the row's member, so at most 256 rows of one device go to one owner, and in every group one owner receives exactly 256 rows from every device of the group.
All inputs are finite; a program needn't handle non-finite values. No bound on the sum of `labels` on one device may be relied on, other than what follows from the above.
Results may differ from the reference program's by a relative error of at most 0.0003.
Values may be sent and summed in bfloat16 or wider, within the bound.
A program may use at most 64 MiB of HBM per device.

```python
import math
import jax
import jax.numpy as jnp
from jax import lax

F = 4096
FR = 256
ROWS_DEV = 1024
MEM_DEV = 8
NEWTON = 2
CG_ITERS = 3
ROWS = 32768
CAP = 256
SLOTS = 2048
GROUP_MEMBERS = 64
MEMBERS = 256
N_GRP = 4
N_MEM = 8


def layout_rows(key):
    base = jax.random.fold_in(key, 7001)

    def one_block(block_key, block):
        group = block // N_MEM
        group_key = jax.random.fold_in(base, 500000 + group)
        key_noise, key_rows, key_first, key_second = jax.random.split(block_key, 4)
        ranking = jax.random.permutation(group_key, N_MEM).astype(jnp.int32)
        owner_of = jnp.arange(SLOTS, dtype=jnp.int32) // CAP
        rank_of = ranking[owner_of]
        noise = jax.random.randint(key_noise, (SLOTS,), 0, 4096, dtype=jnp.int32)
        priority = jnp.where(rank_of == 0, noise - 4096, noise * (1 + rank_of))
        keyed = priority * SLOTS + jnp.arange(SLOTS, dtype=jnp.int32)
        picked = jnp.argsort(keyed)[:ROWS_DEV].astype(jnp.int32)
        shuffle = jax.random.permutation(key_rows, ROWS_DEV).astype(jnp.int32)
        slot_rows = picked[shuffle]
        local_id = jnp.minimum(jax.random.randint(key_first, (ROWS_DEV,), 0, MEM_DEV, dtype=jnp.int32), jax.random.randint(key_second, (ROWS_DEV,), 0, MEM_DEV, dtype=jnp.int32))
        member_rows = group * GROUP_MEMBERS + slot_rows // CAP * MEM_DEV + local_id
        return (member_rows.astype(jnp.int32), slot_rows)
    block_keys = jax.random.split(base, N_GRP * N_MEM)
    members, slots = jax.vmap(one_block)(block_keys, jnp.arange(N_GRP * N_MEM, dtype=jnp.int32))
    return (members.reshape(-1), slots.reshape(-1))


def draw_member_id(key, part):
    return layout_rows(key)[0]


def draw_slot(key, part):
    return layout_rows(key)[1]


def with_ends(values, rng, smallest, top_value):
    longest = values.shape.index(max(values.shape))
    spots = []
    for shift in (0, 1):
        where = [jax.random.randint(jax.random.fold_in(rng, axis), (), 0, length) for axis, length in enumerate(values.shape)]
        where[longest] = (where[longest] + shift) % values.shape[longest]
        spots.append(tuple(where))
    return values.at[spots[0]].set(smallest).at[spots[1]].set(top_value)


def levels(key, extent, pieces, low, top_value):
    level = 1.0
    for axis_at, shards_of in pieces:
        steps = jax.random.uniform(jax.random.fold_in(jax.random.fold_in(key, 6), axis_at), (shards_of,), jnp.float32, low / len(pieces), top_value / len(pieces))
        level = level * jnp.repeat(jnp.exp(steps), extent[axis_at] // shards_of).reshape((-1,) + (1,) * (len(extent) - 1 - axis_at))
    return level


def normal_values(rng, dims, scale, reach, cuts=(), held_as=jnp.bfloat16):
    gain = levels(rng, dims, cuts, -0.22, 0.18) if cuts else 1.0
    array = jax.random.normal(rng, dims, jnp.float32) * scale * gain
    return jnp.minimum(jnp.maximum(array, -reach), reach).astype(held_as)


def setup_inputs(seed: int = 0) -> dict:
    splits = jax.random.split(jax.random.key(seed), 9)
    return {
        "features": normal_values(splits[0], (ROWS, F), F ** -0.5, 0.09375, ((0, 32),)),
        "re_features": normal_values(splits[1], (ROWS, FR), 1.0, 6.0, ((0, 32),)),
        "member_id": draw_member_id(jax.random.fold_in(splits[8], 71), 0),
        "slot": draw_slot(jax.random.fold_in(splits[8], 71), 0),
        "labels": with_ends((jax.random.randint(splits[4], (ROWS,), 0, 2) < 1).astype(jnp.int32), jax.random.fold_in(splits[4], 1), 0, 1),
        "offsets": normal_values(splits[5], (ROWS,), 1.0, 6.0, ((0, 32),), jnp.float32),
        "feature_scale": jnp.clip(jnp.exp(jax.random.uniform(splits[6], (F,), jnp.float32, math.log(0.3), math.log(3.0))), 0.3, 3.0),
        "w_start": normal_values(splits[7], (F,), 0.5, 4.0, (), jnp.float32),
    }


ridge_fixed = 1.0
ridge_member = 1.0

def split_pair(values):
    upper_part = values.astype(jnp.bfloat16)
    held_part = lax.optimization_barrier(upper_part)
    lower_part = (values - held_part.astype(jnp.float32)).astype(jnp.bfloat16)
    return (upper_part, lower_part)

def split_two(vector):
    upper_part, lower_part = split_pair(vector)
    return jnp.stack([upper_part, lower_part], axis=1)

def apply_rows(features, vector):
    return jnp.sum(jnp.dot(features.astype(jnp.float32), split_two(vector).astype(jnp.float32), preferred_element_type=jnp.float32), axis=1)

def apply_columns(features, values):
    pair_cols = split_two(values)
    product = lax.dot_general(pair_cols.astype(jnp.float32), features.astype(jnp.float32), (((0,), (0,)), ((), ())), preferred_element_type=jnp.float32)
    return jnp.sum(product, axis=0)

def inner_rows(left, right):
    return lax.dot_general(left.astype(jnp.float32), right.astype(jnp.float32), (((0,), (0,)), ((), ())), preferred_element_type=jnp.float32)

def fit_members(received, arrived):
    curv_row = arrived[0]
    resid_row = arrived[1]
    local_row = arrived[2]
    onehot = (local_row[:, None] == jnp.arange(MEM_DEV).astype(arrived.dtype)[None, :]).astype(arrived.dtype)
    z_float = received.astype(jnp.float32)

    def gram_one(column):
        upper_part, lower_part = split_pair(z_float * (curv_row * column)[:, None])
        return inner_rows(received, upper_part) + inner_rows(received, lower_part)
    gram_all = lax.map(gram_one, onehot.T) + ridge_member * jnp.eye(received.shape[1], dtype=jnp.float32)
    grad_upper, grad_lower = split_pair(resid_row[:, None] * onehot)
    member_grad = inner_rows(grad_upper, received) + inner_rows(grad_lower, received)
    factor = jnp.linalg.cholesky(gram_all)
    member_coef = -jax.scipy.linalg.cho_solve((factor, True), member_grad[:, :, None])[:, :, 0]
    coef_upper, coef_lower = split_pair(member_coef)
    scores = jnp.dot(received.astype(jnp.float32), coef_upper.T.astype(jnp.float32), preferred_element_type=jnp.float32) + jnp.dot(received.astype(jnp.float32), coef_lower.T.astype(jnp.float32), preferred_element_type=jnp.float32)
    return (member_coef, jnp.sum(scores * onehot, axis=1))

def reference(features, re_features, member_id, slot, labels, offsets, feature_scale, w_start):
    target = labels.astype(jnp.float32)
    weights = w_start
    for newton_step in range(NEWTON):
        margin = apply_rows(features, feature_scale * weights) + offsets
        probability = jax.nn.sigmoid(margin)
        curvature = probability * (1.0 - probability)
        gradient = feature_scale * apply_columns(features, probability - target) + ridge_fixed * weights
        residual = -gradient
        direction = residual
        res_norm = jnp.sum(residual * residual)
        update = jnp.zeros_like(weights)
        for cg_step in range(CG_ITERS):
            inner = curvature * apply_rows(features, feature_scale * direction)
            hess_image = feature_scale * apply_columns(features, inner) + ridge_fixed * direction
            step_size = res_norm / jnp.sum(direction * hess_image)
            update = update + step_size * direction
            residual = residual - step_size * hess_image
            next_norm = jnp.sum(residual * residual)
            direction = residual + next_norm / res_norm * direction
            res_norm = next_norm
        weights = weights + update
    score = apply_rows(features, feature_scale * weights)
    probability = jax.nn.sigmoid(score)
    curvature = probability * (1.0 - probability)
    resid_row = probability - target
    local_id = (member_id % MEM_DEV).astype(jnp.float32)
    row_weights = jnp.stack([curvature, resid_row, local_id], axis=1)
    device_of = (jnp.arange(ROWS, dtype=jnp.int32) // ROWS_DEV).astype(jnp.int32)
    flat_slot = (device_of * SLOTS + slot).astype(jnp.int32)
    owners_all = N_GRP * N_MEM
    z_buffer = jnp.zeros((owners_all * SLOTS, FR), re_features.dtype).at[flat_slot].set(re_features)
    w_buffer = jnp.zeros((owners_all * SLOTS, 3), jnp.float32).at[flat_slot].set(row_weights)
    z_owner = z_buffer.reshape(N_GRP, N_MEM, N_MEM, CAP, FR).transpose(0, 2, 1, 3, 4).reshape(owners_all, SLOTS, FR)
    w_owner = w_buffer.reshape(N_GRP, N_MEM, N_MEM, CAP, 3).transpose(0, 2, 1, 3, 4).reshape(owners_all, SLOTS, 3)
    all_coef, slot_scores = lax.map(lambda pair_in: fit_members(pair_in[0], pair_in[1].T), (z_owner, w_owner))
    back_flat = slot_scores.reshape(N_GRP, N_MEM, N_MEM, CAP).transpose(0, 2, 1, 3).reshape(-1)
    row_offsets = back_flat[flat_slot]
    return (weights, all_coef.reshape(MEMBERS, FR), row_offsets)
```

```python
import functools

import jax
import jax.numpy as jnp
from jax import lax
from jax.experimental import pallas as pl
from jax.experimental.pallas import tpu as pltpu
from jax.sharding import PartitionSpec as P

MEM_DEV = 8
NEWTON = 2
CG_ITERS = 3
LANES = 128
BLOCK = 32

ridge_fixed = 1.0
ridge_member = 1.0
MESH_ID = pl.DeviceIdType.MESH
NT = (((1,), (1,)), ((), ()))
NN = (((1,), (0,)), ((), ()))
TN = (((0,), (0,)), ((), ()))


def pair_rows(row):
    upper = row.astype(jnp.bfloat16).astype(jnp.float32)
    lower = (row - upper).astype(jnp.bfloat16).astype(jnp.float32)
    at = lax.broadcasted_iota(jnp.int32, (16, row.shape[1]), 0)
    both = jnp.where(at == 0, upper, jnp.where(at == 1, lower, 0.0))
    return both.astype(jnp.bfloat16)


def three_parts(value):
    first = value.astype(jnp.bfloat16)
    rest = value - first.astype(jnp.float32)
    second = rest.astype(jnp.bfloat16)
    third = (rest - second.astype(jnp.float32)).astype(jnp.bfloat16)
    return first, second, third


def invert_blocks(blocks):
    lane = lax.broadcasted_iota(jnp.int32, (BLOCK, LANES), 1)
    sub = lax.broadcasted_iota(jnp.int32, (BLOCK, LANES), 0)
    base = lane // BLOCK * BLOCK
    place = lane % BLOCK
    for k in range(0, BLOCK, 2):
        one, two = place == k, place == k + 1
        new = []
        for value in blocks:
            left = jnp.take_along_axis(value, base + k, axis=1)
            right = jnp.take_along_axis(value, base + k + 1, axis=1)
            a, b = left[k : k + 1, :], right[k : k + 1, :]
            c, d = left[k + 1 : k + 2, :], right[k + 1 : k + 2, :]
            inverse = 1.0 / (a * d - b * c)
            a, b, c, d = d * inverse, -b * inverse, -c * inverse, a * inverse
            top, low = value[k : k + 1, :], value[k + 1 : k + 2, :]
            at_one, at_two = one[0:1, :], two[0:1, :]
            first = jnp.where(at_one, a, jnp.where(at_two, b, a * top + b * low))
            second = jnp.where(at_one, c, jnp.where(at_two, d, c * top + d * low))
            value = jnp.where(one | two, 0.0, value) - left * first - right * second
            value = jnp.where(sub == k, first, jnp.where(sub == k + 1, second, value))
            new.append(value)
        blocks = new
        yield blocks


def fit_members(z_ref, zt_ref, curv_row, resid_row, local, coef_ref, gram, upper, lower):
    width = z_ref.shape[1]
    slots = z_ref.shape[0]
    count = coef_ref.shape[0]
    per = LANES // BLOCK
    blocks = width // BLOCK
    weighted = zt_ref[...].astype(jnp.float32) * curv_row
    first = weighted.astype(jnp.bfloat16)
    upper[...] = first
    lower[...] = (weighted - first.astype(jnp.float32)).astype(jnp.bfloat16)
    eye = (
        lax.broadcasted_iota(jnp.int32, (width, width), 0)
        == lax.broadcasted_iota(jnp.int32, (width, width), 1)
    ).astype(jnp.float32)

    @pl.loop(0, count)
    def _(m):
        mask = jnp.where(local == m.astype(jnp.float32), 1.0, 0.0).astype(jnp.bfloat16)
        total = lax.dot_general(
            upper[...] * mask, z_ref[...], NN, preferred_element_type=jnp.float32
        ) + lax.dot_general(
            lower[...] * mask, z_ref[...], NN, preferred_element_type=jnp.float32
        )
        gram[m] = total + ridge_member * eye

    member = lax.broadcasted_iota(jnp.int32, (count, slots), 0).astype(jnp.float32)
    own = member == local
    masked = jnp.where(own, resid_row, 0.0)
    high = masked.astype(jnp.bfloat16)
    low = (masked - high.astype(jnp.float32)).astype(jnp.bfloat16)
    grad = lax.dot_general(
        high, z_ref[...], NN, preferred_element_type=jnp.float32
    ) + lax.dot_general(low, z_ref[...], NN, preferred_element_type=jnp.float32)
    rhs = [grad[m : m + 1, :] for m in range(count)]
    exact = dict(preferred_element_type=jnp.float32, precision=lax.Precision.HIGHEST)
    inverse_of = []
    heads = {}
    rows_now = [gram[m, 0:BLOCK, :] for m in range(count)]
    start = 0
    later = []

    def trailing(m, first, start, left_cat, right_cat):
        update = lax.dot_general(left_cat, right_cat, TN, preferred_element_type=jnp.float32)
        gram[m, first:width, start:width] = gram[m, first:width, start:width] - update[first - start :]

    for b in range(blocks):
        lo, hi = b * BLOCK, (b + 1) * BLOCK
        squares = [rows_now[m][:, lo - start : hi - start] for m in range(count)]
        packed = [
            jnp.concatenate(squares[at : at + per], axis=1) for at in range(0, count, per)
        ]
        for step, packed in enumerate(invert_blocks(packed)):
            if later and step % 2 == 1:
                later.pop(0)()
        while later:
            later.pop(0)()
        inverses = [
            packed[m // per][:, m % per * BLOCK : (m % per + 1) * BLOCK] for m in range(count)
        ]
        panels = []
        following = []
        new_start = hi // LANES * LANES
        for m in range(count):
            head = rhs[m][:, lo - start : hi - start]
            heads[(m, b)] = head
            if hi == width:
                continue
            right = rows_now[m][:, new_start - start :]
            panel = lax.dot_general(inverses[m], right, NN, **exact)
            panels.append(panel)
            a1, a2, a3 = three_parts(right)
            b1, b2, b3 = three_parts(panel)
            left_cat = jnp.concatenate([a1, a1, a2, a2, a1, a3], axis=0)
            right_cat = jnp.concatenate([b1, b2, b1, b2, b3, b1], axis=0)
            skip = hi - new_start
            following.append(
                gram[m, hi : hi + BLOCK, new_start:width]
                - lax.dot_general(
                    left_cat[:, skip : skip + BLOCK],
                    right_cat,
                    TN,
                    preferred_element_type=jnp.float32,
                )
            )
            if hi + BLOCK < width:
                later.append(
                    functools.partial(trailing, m, hi + BLOCK, new_start, left_cat, right_cat)
                )
            rhs[m] = rhs[m][:, new_start - start :] - lax.dot_general(head, panel, NN, **exact)
        rows_now = following
        inverse_of.append((inverses, panels, new_start))
        start = new_start
    pieces = [[None] * blocks for _ in range(count)]
    for b in reversed(range(blocks)):
        inverses, panels, begin = inverse_of[b]
        for m in range(count):
            part = lax.dot_general(heads[(m, b)], inverses[m], NN, **exact)
            if panels:
                gap = (b + 1) * BLOCK - begin
                tail = ([jnp.zeros((1, gap), jnp.float32)] if gap else []) + pieces[m][b + 1 :]
                tail = jnp.concatenate(tail, axis=1) if len(tail) > 1 else tail[0]
                part = part - lax.dot_general(tail, panels[m], NT, **exact)
            pieces[m][b] = part
    solved = [jnp.concatenate(pieces[m], axis=1) for m in range(count)]
    coef = -jnp.concatenate(solved, axis=0)
    coef_ref[...] = coef
    high = coef.astype(jnp.bfloat16)
    low = (coef - high.astype(jnp.float32)).astype(jnp.bfloat16)
    scores = lax.dot_general(
        high, zt_ref[...], NN, preferred_element_type=jnp.float32
    ) + lax.dot_general(low, zt_ref[...], NN, preferred_element_type=jnp.float32)
    return jnp.sum(jnp.where(own, scores, 0.0), axis=0, keepdims=True)


def window_kernel(
    n_grp, n_mem,
    feat_hbm, re_hbm, member_hbm, slot_hbm, label_hbm, offset_hbm, scale_hbm, start_hbm,
    weight_ref, coef_ref, offsets_ref,
    feat, re_ref, member_ref, slot_ref, label_ref, offset_ref, scale_ref, vec_w,
    vec_u, vec_r, vec_p, curv, score, near_send, near_recv, far_send, far_recv, one_send, one_recv,
    pick, z_send, z_ref, zs_ref, zt_ref, w_send, w_recv, s_send, s_recv, gram, upper, lower, row_vals,
    load_sem, feat_sem, ns_sem, nr_sem, fs_sem, fr_sem, os_sem, or_sem, zs_sem, zr_sem, ws_sem, wr_sem, ss_sem, sr_sem,
):
    rows, width = feat.shape
    lines = width // LANES
    slots = z_ref.shape[0]
    cap = slots // n_mem
    calls = NEWTON * (CG_ITERS + 1)
    each = n_mem // calls
    direct = n_grp * n_mem <= 32
    me_grp = lax.axis_index("grp")
    me_mem = lax.axis_index("mem")

    loads = [
        pltpu.make_async_copy(source, target, load_sem.at[i])
        for i, (source, target) in enumerate(
            (
                (scale_hbm, scale_ref), (start_hbm, vec_w), (offset_hbm, offset_ref),
                (label_hbm, label_ref), (slot_hbm, slot_ref), (member_hbm, member_ref),
                (re_hbm, re_ref),
            )
        )
    ]
    feat_loads = [
        pltpu.make_async_copy(
            feat_hbm.at[pl.ds(first, 256)], feat.at[pl.ds(first, 256)], feat_sem.at[first // 256]
        )
        for first in range(0, rows, 256)
    ]
    for load in loads[:4] + feat_loads + loads[4:]:
        load.start()

    low = 2
    high = n_mem // low
    near = n_grp * low
    me_low = lax.rem(me_mem, low)
    me_high = me_mem // low
    me_near = me_grp * low + me_low

    def near_peer(turn):
        other = lax.rem(me_near + turn, near)
        return (other // low, me_high * low + lax.rem(other, low))

    def far_peer(turn):
        return (me_grp, lax.rem(me_high + turn, high) * low + me_low)

    me_all = me_grp * n_mem + me_mem

    def any_peer(turn):
        other = lax.rem(me_all + turn, n_grp * n_mem)
        return (other // n_mem, lax.rem(other, n_mem))

    barrier = pltpu.get_barrier_semaphore()
    if direct:
        for turn in range(1, n_grp * n_mem):
            pl.semaphore_signal(barrier, inc=1, device_id=any_peer(turn), device_id_type=MESH_ID)
        pl.semaphore_wait(barrier, n_grp * n_mem - 1)
    else:
        for turn in range(1, n_mem):
            pl.semaphore_signal(
                barrier, inc=1, device_id=(me_grp, lax.rem(me_mem + turn, n_mem)), device_id_type=MESH_ID
            )
        for turn in range(1, near):
            pl.semaphore_signal(barrier, inc=1, device_id=near_peer(turn), device_id_type=MESH_ID)
        pl.semaphore_wait(barrier, n_mem - 1 + near - 1)
    for load in loads[:4]:
        load.wait()

    def peer(turn):
        return (me_grp, lax.rem(me_mem + turn, n_mem))

    def z_copy(turn):
        return pltpu.make_async_remote_copy(
            src_ref=z_send.at[turn - 1],
            dst_ref=z_ref.at[pl.ds(pl.multiple_of(me_mem * cap, cap), cap)],
            send_sem=zs_sem.at[turn - 1],
            recv_sem=zr_sem.at[turn - 1],
            device_id=peer(turn),
            device_id_type=MESH_ID,
        )

    def build(turn):
        first = pl.multiple_of(lax.rem(me_mem + turn, n_mem) * cap, cap)
        at = lax.broadcasted_iota(jnp.int32, (cap, rows), 0) + first
        chosen = jnp.where(at == slot_ref[...], 1.0, 0.0).astype(jnp.bfloat16)
        pick[pl.ds(first, cap), :] = chosen
        block = lax.dot_general(chosen, re_ref[...], NN, preferred_element_type=jnp.float32)
        block = block.astype(jnp.bfloat16)

        @pl.when(turn < n_mem)
        def _():
            z_send[turn - 1] = block

        @pl.when(turn == n_mem)
        def _():
            z_ref[pl.ds(pl.multiple_of(me_mem * cap, cap), cap), :] = block

    def exchange(value, call, size, me, peer_of, source, slots_of, sends, recvs, between=None):
        source[call] = value
        for turn in range(1, size):
            pltpu.make_async_remote_copy(
                src_ref=source.at[call],
                dst_ref=slots_of.at[call, me],
                send_sem=sends.at[call],
                recv_sem=recvs.at[call],
                device_id=peer_of(turn),
                device_id_type=MESH_ID,
            ).start()
        slots_of[call, me] = value
        if between is not None:
            between()
        others = slots_of.at[call, pl.ds(0, size - 1)]
        pltpu.make_async_copy(others, others, recvs.at[call]).wait()
        pltpu.make_async_copy(others, others, sends.at[call]).wait()
        parts = [slots_of[call, i] for i in range(size)]
        while len(parts) > 1:
            parts = [parts[i] + parts[i + 1] for i in range(0, len(parts), 2)]
        return parts[0]

    def regroup(call):
        for q in range(each):
            build(1 + call * each + q)

    def forward(call):
        for q in range(each):
            turn = 1 + call * each + q

            @pl.when(turn < n_mem)
            def _():
                z_copy(turn).start()

    def all_sum(value, call, fill):
        value = exchange(
            value, call, near, me_near, near_peer, near_send, near_recv, ns_sem, nr_sem,
            functools.partial(regroup, fill),
        )
        value = exchange(
            value, call, high, me_high, far_peer, far_send, far_recv, fs_sem, fr_sem
        )
        forward(fill)
        return value

    def small_sum(value, call, fill):
        value = jnp.broadcast_to(value, (1, LANES))
        if direct:
            value = exchange(
                value, call, n_grp * n_mem, me_all, any_peer, one_send, one_recv, os_sem, or_sem,
                functools.partial(regroup, fill),
            )
            forward(fill)
            return value[:, 0:1]
        wide = jnp.broadcast_to(value, (lines, LANES))
        return all_sum(wide, NEWTON * CG_ITERS + call, fill)[0:1, 0:1]

    def times_rows(vector, loading=False):
        row = jnp.concatenate([vector[i : i + 1, :] for i in range(lines)], axis=1)
        pair = pair_rows(row)
        parts = []
        for first in range(0, rows, 256):
            if loading:
                feat_loads[first // 256].wait()
            got = lax.dot_general(
                pair, feat[first : first + 256, :], NT, preferred_element_type=jnp.float32
            )
            parts.append(got[0:1] + got[1:2])
        return jnp.concatenate(parts, axis=1)

    def times_columns(row):
        pair = pair_rows(row)
        parts = []
        for first in range(0, width, 256):
            got = lax.dot_general(
                pair, feat[:, first : first + 256], NN, preferred_element_type=jnp.float32
            )
            got = got[0:1] + got[1:2]
            parts += [got[:, at : at + LANES] for at in range(0, 256, LANES)]
        return jnp.concatenate(parts, axis=0)

    def total(value):
        return jnp.sum(jnp.sum(value, axis=1, keepdims=True), axis=0, keepdims=True)

    scale = scale_ref[...]
    target = label_ref[...].astype(jnp.float32)

    score[...] = times_rows(scale * vec_w[...], True)

    def newton(step, carry):
        weights = vec_w[...]
        margin = score[...] + offset_ref[...]
        prob = 1.0 / (1.0 + jnp.exp(-margin))
        curv[...] = prob * (1.0 - prob)
        grad = times_columns(prob - target)

        @pl.when(step == 0)
        def _():
            for load in loads[4:]:
                load.wait()

        base = step * CG_ITERS
        fill = step * (CG_ITERS + 1)
        resid = -(scale * all_sum(grad, base, fill) + ridge_fixed * weights)
        vec_r[...] = resid
        vec_p[...] = resid
        vec_u[...] = jnp.zeros_like(resid)

        def cg(k, norm):
            direction = vec_p[...]
            along = times_rows(scale * direction)
            image = all_sum(times_columns(curv[...] * along), base + 1 + k, fill + 1 + k)
            image = scale * image + ridge_fixed * direction
            size = norm / total(direction * image)
            vec_u[...] = vec_u[...] + size * direction
            score[...] = score[...] + size * along
            left = vec_r[...] - size * image
            vec_r[...] = left
            new_norm = total(left * left)
            vec_p[...] = left + new_norm / norm * direction
            return new_norm

        norm = lax.fori_loop(0, CG_ITERS - 1, cg, total(resid * resid))
        direction = vec_p[...]
        along = times_rows(scale * direction)
        bend = small_sum(total(curv[...] * along * along), step, fill + CG_ITERS)
        size = norm / (bend + ridge_fixed * total(direction * direction))
        score[...] = score[...] + size * along
        vec_w[...] = weights + (vec_u[...] + size * direction)
        return carry

    lax.fori_loop(0, NEWTON, newton, 0)
    weight_ref[...] = vec_w[...]
    prob = 1.0 / (1.0 + jnp.exp(-score[...]))
    local_id = lax.rem(member_ref[...], MEM_DEV).astype(jnp.float32)
    row_vals[...] = jnp.zeros_like(row_vals)
    row_vals[0:1, :] = prob * (1.0 - prob)
    row_vals[1:2, :] = prob - target
    row_vals[2:3, :] = local_id
    parts = jnp.concatenate([p.astype(jnp.float32) for p in three_parts(row_vals[...])], axis=0)
    parts = jnp.concatenate([parts, jnp.zeros_like(parts[0:8])], axis=0).astype(jnp.bfloat16)

    def small_copy(source, target, turn, sends, recvs):
        return pltpu.make_async_remote_copy(
            src_ref=source.at[turn - 1],
            dst_ref=target.at[turn - 1],
            send_sem=sends.at[turn - 1],
            recv_sem=recvs.at[turn - 1],
            device_id=peer(turn),
            device_id_type=MESH_ID,
        )

    for turn in range(1, n_mem + 1):
        first = pl.multiple_of(lax.rem(me_mem + turn, n_mem) * cap, cap)
        got = lax.dot_general(
            parts, pick[pl.ds(first, cap), :], NT, preferred_element_type=jnp.float32
        )
        got = got[0:8] + got[8:16] + got[16:24]
        if turn < n_mem:
            w_send[turn - 1] = got
            small_copy(w_send, w_recv, turn, ws_sem, wr_sem).start()
        else:
            w_recv[n_mem - 1] = got
    for turn in range(1, n_mem):
        z_copy(turn).wait()
    for turn in range(1, n_mem + 1):
        source = lax.rem(me_mem + n_mem - turn, n_mem)
        block = z_ref[pl.ds(pl.multiple_of(source * cap, cap), cap), :]
        zt_ref[:, (turn - 1) * cap : turn * cap] = block.T
        zs_ref[(turn - 1) * cap : turn * cap, :] = block
    for turn in range(1, n_mem):
        small_copy(w_send, w_recv, turn, ws_sem, wr_sem).wait()
    arrived = jnp.concatenate([w_recv[t] for t in range(n_mem)], axis=1)
    scores = fit_members(
        zs_ref, zt_ref, arrived[0:1], arrived[1:2], arrived[2:3], coef_ref, gram, upper, lower
    )
    for turn in range(1, n_mem + 1):
        back = jnp.broadcast_to(scores[:, (turn - 1) * cap : turn * cap], (8, cap))
        if turn < n_mem:
            s_send[n_mem - turn - 1] = back
        else:
            s_recv[n_mem - 1] = back
    for turn in range(1, n_mem):
        small_copy(s_send, s_recv, turn, ss_sem, sr_sem).start()
    for turn in range(1, n_mem):
        small_copy(s_send, s_recv, turn, ss_sem, sr_sem).wait()
    result = jnp.zeros((1, rows), jnp.float32)
    for turn in range(1, n_mem + 1):
        owner = lax.rem(me_mem + n_mem - turn, n_mem)
        value = s_recv[turn - 1][0:1]
        p1, p2, p3 = (p.astype(jnp.float32) for p in three_parts(value))
        at = lax.broadcasted_iota(jnp.int32, (16, cap), 0)
        stack = jnp.where(at == 0, p1, jnp.where(at == 1, p2, jnp.where(at == 2, p3, 0.0)))
        got = lax.dot_general(
            stack.astype(jnp.bfloat16),
            pick[pl.ds(pl.multiple_of(owner * cap, cap), cap), :],
            NN,
            preferred_element_type=jnp.float32,
        )
        result = result + (got[0:1] + got[1:2] + got[2:3])
    offsets_ref[...] = result


def on_device(n_grp, n_mem, features, re_features, member_id, slot, labels, offsets, feature_scale, w_start):
    rows, width = features.shape
    inner = re_features.shape[1]
    lines = width // LANES
    slots = 2 * rows
    cap = slots // n_mem
    near, high = 2 * n_grp, n_mem // 2
    direct = n_grp * n_mem <= 32
    calls = NEWTON * CG_ITERS if direct else NEWTON * (CG_ITERS + 1)
    every = n_grp * n_mem if direct else 2
    f32, bf16, i32 = jnp.float32, jnp.bfloat16, jnp.int32
    held = pltpu.VMEM((lines, LANES), f32)
    dma = pltpu.SemaphoreType.DMA
    whole = pl.BlockSpec(memory_space=pltpu.VMEM)
    weights, member_coef, row_offsets = pl.pallas_call(
        functools.partial(window_kernel, n_grp, n_mem),
        out_shape=(
            jax.ShapeDtypeStruct((lines, LANES), f32),
            jax.ShapeDtypeStruct((MEM_DEV, inner), f32),
            jax.ShapeDtypeStruct((1, rows), f32),
        ),
        in_specs=[pl.BlockSpec(memory_space=pl.ANY)] * 8,
        out_specs=(whole,) * 3,
        scratch_shapes=[
            pltpu.VMEM((rows, width), bf16),
            pltpu.VMEM((rows, inner), bf16),
            pltpu.VMEM((1, rows), i32),
            pltpu.VMEM((1, rows), i32),
            pltpu.VMEM((1, rows), i32),
            pltpu.VMEM((1, rows), f32),
            held, held, held, held, held,
            pltpu.VMEM((1, rows), f32),
            pltpu.VMEM((1, rows), f32),
            pltpu.VMEM((calls, lines, LANES), f32),
            pltpu.VMEM((calls, near, lines, LANES), f32),
            pltpu.VMEM((calls, lines, LANES), f32),
            pltpu.VMEM((calls, high, lines, LANES), f32),
            pltpu.VMEM((NEWTON, 1, LANES), f32),
            pltpu.VMEM((NEWTON, every, 1, LANES), f32),
            pltpu.VMEM((slots, rows), bf16),
            pltpu.VMEM((n_mem - 1, cap, inner), bf16),
            pltpu.VMEM((slots, inner), bf16),
            pltpu.VMEM((slots, inner), bf16),
            pltpu.VMEM((inner, slots), bf16),
            pltpu.VMEM((n_mem - 1, 8, cap), f32),
            pltpu.VMEM((n_mem, 8, cap), f32),
            pltpu.VMEM((n_mem - 1, 8, cap), f32),
            pltpu.VMEM((n_mem, 8, cap), f32),
            pltpu.VMEM((MEM_DEV, inner, inner), f32),
            pltpu.VMEM((inner, slots), bf16),
            pltpu.VMEM((inner, slots), bf16),
            pltpu.VMEM((8, rows), f32),
            dma((7,)),
            dma((rows // 256,)),
            dma((calls,)),
            dma((calls,)),
            dma((calls,)),
            dma((calls,)),
            dma((NEWTON,)),
            dma((NEWTON,)),
            dma((n_mem - 1,)),
            dma((n_mem - 1,)),
            dma((n_mem - 1,)),
            dma((n_mem - 1,)),
            dma((n_mem - 1,)),
            dma((n_mem - 1,)),
        ],
        compiler_params=pltpu.CompilerParams(
            collective_id=0, has_side_effects=True, vmem_limit_bytes=60 << 20
        ),
        name="window",
    )(
        features,
        re_features,
        member_id.reshape(1, rows),
        slot.reshape(1, rows),
        labels.reshape(1, rows),
        offsets.reshape(1, rows),
        feature_scale.reshape(lines, LANES),
        w_start.reshape(lines, LANES),
    )
    return (weights.reshape(-1), member_coef, row_offsets.reshape(-1))


def solution(mesh):
    placed = (
        P(("grp", "mem"), None),
        P(("grp", "mem"), None),
        P(("grp", "mem")),
        P(("grp", "mem")),
        P(("grp", "mem")),
        P(("grp", "mem")),
        P(),
        P(),
    )
    return jax.shard_map(
        functools.partial(on_device, mesh.shape["grp"], mesh.shape["mem"]),
        mesh=mesh,
        in_specs=placed,
        out_specs=(P(), P(("grp", "mem"), None), P(("grp", "mem"))),
        check_vma=False,
    )
```

```python
import functools

import jax
import jax.numpy as jnp
from jax import lax
from jax.experimental import pallas as pl
from jax.experimental.pallas import tpu as pltpu
from jax.sharding import PartitionSpec as P

MEM_DEV = 8
NEWTON = 2
CG_ITERS = 3
LANES = 128
BLOCK = 32
BUILD_CALLS = 4

ridge_fixed = 1.0
ridge_member = 1.0
MESH_ID = pl.DeviceIdType.MESH
NT = (((1,), (1,)), ((), ()))
NN = (((1,), (0,)), ((), ()))
TN = (((0,), (0,)), ((), ()))


def pair_rows(row):
    upper = row.astype(jnp.bfloat16).astype(jnp.float32)
    lower = (row - upper).astype(jnp.bfloat16).astype(jnp.float32)
    at = lax.broadcasted_iota(jnp.int32, (16, row.shape[1]), 0)
    both = jnp.where(at == 0, upper, jnp.where(at == 1, lower, 0.0))
    return both.astype(jnp.bfloat16)


def three_parts(value):
    first = value.astype(jnp.bfloat16)
    rest = value - first.astype(jnp.float32)
    second = rest.astype(jnp.bfloat16)
    third = (rest - second.astype(jnp.float32)).astype(jnp.bfloat16)
    return first, second, third


def split_six(value, axis, left):
    first, second, third = three_parts(value)
    if left:
        return jnp.concatenate([first, first, second, second, first, third], axis=axis)
    return jnp.concatenate([first, second, first, second, third, first], axis=axis)


def invert_blocks(blocks):
    lane = lax.broadcasted_iota(jnp.int32, (BLOCK, LANES), 1)
    sub = lax.broadcasted_iota(jnp.int32, (BLOCK, LANES), 0)
    base = lane // BLOCK * BLOCK
    place = lane % BLOCK

    def column(value, k):
        return jnp.take_along_axis(value, base + k, axis=1)

    blocks = [(value, column(value, 0), column(value, 1)) for value in blocks]
    for k in range(0, BLOCK, 2):
        one, two = place == k, place == k + 1
        at_one, at_two = one[0:1, :], two[0:1, :]
        new = []
        for value, left, right in blocks:
            ahead = [column(value, k + 2), column(value, k + 3)] if k + 2 < BLOCK else []
            a, b = left[k : k + 1, :], right[k : k + 1, :]
            c, d = left[k + 1 : k + 2, :], right[k + 1 : k + 2, :]
            inverse = 1.0 / (a * d - b * c)
            a, b, c, d = d * inverse, -b * inverse, -c * inverse, a * inverse

            def update(value, first, second):
                value = value - left * first - right * second
                return jnp.where(sub == k, first, jnp.where(sub == k + 1, second, value))

            following = []
            for col in ahead:
                top, low = col[k : k + 1, :], col[k + 1 : k + 2, :]
                following.append(update(col, a * top + b * low, c * top + d * low))
            top, low = value[k : k + 1, :], value[k + 1 : k + 2, :]
            first = jnp.where(at_one, a, jnp.where(at_two, b, a * top + b * low))
            second = jnp.where(at_one, c, jnp.where(at_two, d, c * top + d * low))
            value = update(jnp.where(one | two, 0.0, value), first, second)
            new.append((value, *(following or (left, right))))
        blocks = new
        yield [value for value, _, _ in blocks]


def fit_members(z_ref, zt_ref, curv_row, resid_row, local, gram, upper, lower):
    width = z_ref.shape[1]
    slots = z_ref.shape[0]
    count = MEM_DEV
    per = LANES // BLOCK
    blocks = width // BLOCK
    weighted = zt_ref[...].astype(jnp.float32) * curv_row
    first = weighted.astype(jnp.bfloat16)
    upper[...] = first
    lower[...] = (weighted - first.astype(jnp.float32)).astype(jnp.bfloat16)
    eye = (
        lax.broadcasted_iota(jnp.int32, (width, width), 0)
        == lax.broadcasted_iota(jnp.int32, (width, width), 1)
    ).astype(jnp.float32)

    @pl.loop(0, count)
    def _(m):
        mask = jnp.where(local == m.astype(jnp.float32), 1.0, 0.0).astype(jnp.bfloat16)
        total = lax.dot_general(
            upper[...] * mask, z_ref[...], NN, preferred_element_type=jnp.float32
        ) + lax.dot_general(
            lower[...] * mask, z_ref[...], NN, preferred_element_type=jnp.float32
        )
        gram[m] = total + ridge_member * eye

    member = lax.broadcasted_iota(jnp.int32, (count, slots), 0).astype(jnp.float32)
    masked = jnp.where(member == local, resid_row, 0.0)
    high = masked.astype(jnp.bfloat16)
    low = (masked - high.astype(jnp.float32)).astype(jnp.bfloat16)
    goal = lax.dot_general(
        high, z_ref[...], NN, preferred_element_type=jnp.float32
    ) + lax.dot_general(low, z_ref[...], NN, preferred_element_type=jnp.float32)

    place = lax.broadcasted_iota(jnp.int32, (1, width), 1)
    turn = lax.broadcasted_iota(jnp.int32, (count, width), 0)
    lane = lax.broadcasted_iota(jnp.int32, (BLOCK, LANES), 1)
    unit = lax.broadcasted_iota(jnp.int32, (BLOCK, width), 1)
    unit = unit - lax.broadcasted_iota(jnp.int32, (BLOCK, width), 0)
    later = []

    def trailing(m, first, inside, left, right):
        update = lax.dot_general(left, right, TN, preferred_element_type=jnp.float32)
        gram[m, first:width, :] = jnp.where(inside, 0.0, gram[m, first:width, :]) - update

    rows_now = [gram[m, 0:BLOCK, :] for m in range(count)]
    for b in range(blocks):
        lo, hi = b * BLOCK, (b + 1) * BLOCK
        packed = [
            jnp.concatenate([rows_now[m][:, lo:hi] for m in range(at, at + per)], axis=1)
            for at in range(0, count, per)
        ]
        for step, packed in enumerate(invert_blocks(packed)):
            if later and step % 2 == 1:
                later.pop(0)()
        while later:
            later.pop(0)()
        inside = (place >= lo) & (place < hi)
        panels = []
        for index, value in enumerate(packed):
            left = jnp.concatenate(
                [jnp.where(lane // BLOCK == i, value, 0.0) for i in range(per)], axis=0
            )
            right = jnp.concatenate(
                [
                    jnp.where(inside, jnp.where(unit == lo, -1.0, 0.0), rows_now[index * per + i])
                    for i in range(per)
                ],
                axis=0,
            )
            got = lax.dot_general(
                split_six(left, 1, True), split_six(right, 0, False), NN,
                preferred_element_type=jnp.float32,
            )
            panels += [got[i * BLOCK : (i + 1) * BLOCK, :] for i in range(per)]
        heads = split_six(goal[:, lo:hi], 1, True)
        goal = jnp.where(inside, 0.0, goal)
        following = []
        for m in range(count):
            right = split_six(panels[m], 0, False)
            if hi < width:
                left = split_six(rows_now[m][:, hi:], 0, True)
                update = lax.dot_general(
                    left[:, 0:BLOCK], right, TN, preferred_element_type=jnp.float32
                )
                following.append(jnp.where(inside, 0.0, gram[m, hi : hi + BLOCK, :]) - update)
                if hi + BLOCK < width:
                    later.append(
                        functools.partial(
                            trailing, m, hi + BLOCK, inside, left[:, BLOCK:], right
                        )
                    )
            update = lax.dot_general(heads, right, NN, preferred_element_type=jnp.float32)
            goal = goal - jnp.where(turn == m, update, 0.0)
        rows_now = following
    return -goal


def window_kernel(
    n_grp, n_mem,
    feat_hbm, re_hbm, member_hbm, slot_hbm, label_hbm, offset_hbm, scale_hbm, start_hbm,
    weight_ref, coef_ref, offsets_ref,
    feat, re_ref, member_ref, slot_ref, label_ref, offset_ref, scale_ref, vec_w,
    vec_u, vec_r, vec_p, curv, score, near_send, near_recv, far_send, far_recv, one_send, one_recv,
    pick, z_send, z_ref, zt_ref, w_send, w_recv, c_recv, gram, upper, lower, row_vals,
    load_sem, feat_sem, ns_sem, nr_sem, fs_sem, fr_sem, os_sem, or_sem, zs_sem, zr_sem, ws_sem, wr_sem, cs_sem, cr_sem,
):
    rows, width = feat.shape
    lines = width // LANES
    slots = z_ref.shape[0]
    cap = slots // n_mem
    each = pl.cdiv(n_mem, BUILD_CALLS)
    direct = n_grp * n_mem <= 32
    me_grp = lax.axis_index("grp")
    me_mem = lax.axis_index("mem")

    loads = [
        pltpu.make_async_copy(source, target, load_sem.at[i])
        for i, (source, target) in enumerate(
            (
                (scale_hbm, scale_ref), (start_hbm, vec_w), (offset_hbm, offset_ref),
                (label_hbm, label_ref), (slot_hbm, slot_ref), (member_hbm, member_ref),
                (re_hbm, re_ref),
            )
        )
    ]
    feat_loads = [
        pltpu.make_async_copy(
            feat_hbm.at[pl.ds(first, 256)], feat.at[pl.ds(first, 256)], feat_sem.at[first // 256]
        )
        for first in range(0, rows, 256)
    ]
    for load in loads[:4] + feat_loads + loads[4:]:
        load.start()

    low = 2
    high = n_mem // low
    near = n_grp * low
    me_low = lax.rem(me_mem, low)
    me_high = me_mem // low
    me_near = me_grp * low + me_low

    def near_peer(turn):
        other = lax.rem(me_near + turn, near)
        return (other // low, me_high * low + lax.rem(other, low))

    def far_peer(turn):
        return (me_grp, lax.rem(me_high + turn, high) * low + me_low)

    me_all = me_grp * n_mem + me_mem

    def any_peer(turn):
        other = lax.rem(me_all + turn, n_grp * n_mem)
        return (other // n_mem, lax.rem(other, n_mem))

    barrier = pltpu.get_barrier_semaphore()
    if direct:
        for turn in range(1, n_grp * n_mem):
            pl.semaphore_signal(barrier, inc=1, device_id=any_peer(turn), device_id_type=MESH_ID)
        pl.semaphore_wait(barrier, n_grp * n_mem - 1)
    else:
        for turn in range(1, n_mem):
            pl.semaphore_signal(
                barrier, inc=1, device_id=(me_grp, lax.rem(me_mem + turn, n_mem)), device_id_type=MESH_ID
            )
        for turn in range(1, near):
            pl.semaphore_signal(barrier, inc=1, device_id=near_peer(turn), device_id_type=MESH_ID)
        pl.semaphore_wait(barrier, n_mem - 1 + near - 1)
    for load in loads[:4]:
        load.wait()

    def peer(turn):
        return (me_grp, lax.rem(me_mem + turn, n_mem))

    def z_copy(turn):
        return pltpu.make_async_remote_copy(
            src_ref=z_send.at[turn - 1],
            dst_ref=z_ref.at[pl.ds(pl.multiple_of((turn - 1) * cap, cap), cap)],
            send_sem=zs_sem.at[turn - 1],
            recv_sem=zr_sem.at[turn - 1],
            device_id=peer(turn),
            device_id_type=MESH_ID,
        )

    def build(turn):
        first = pl.multiple_of(lax.rem(me_mem + turn, n_mem) * cap, cap)
        at = lax.broadcasted_iota(jnp.int32, (cap, rows), 0) + first
        chosen = jnp.where(at == slot_ref[...], 1.0, 0.0).astype(jnp.bfloat16)
        pick[pl.ds(first, cap), :] = chosen
        block = lax.dot_general(chosen, re_ref[...], NN, preferred_element_type=jnp.float32)
        block = block.astype(jnp.bfloat16)

        @pl.when(turn < n_mem)
        def _():
            z_send[turn - 1] = block

        @pl.when(turn == n_mem)
        def _():
            z_ref[(n_mem - 1) * cap :, :] = block

    def exchange(value, call, size, me, peer_of, source, slots_of, sends, recvs, between=None):
        source[call] = value
        for turn in range(1, size):
            pltpu.make_async_remote_copy(
                src_ref=source.at[call],
                dst_ref=slots_of.at[call, me],
                send_sem=sends.at[call],
                recv_sem=recvs.at[call],
                device_id=peer_of(turn),
                device_id_type=MESH_ID,
            ).start()
        slots_of[call, me] = value
        if between is not None:
            between()
        others = slots_of.at[call, pl.ds(0, size - 1)]
        pltpu.make_async_copy(others, others, recvs.at[call]).wait()
        pltpu.make_async_copy(others, others, sends.at[call]).wait()
        parts = [slots_of[call, i] for i in range(size)]
        while len(parts) > 1:
            parts = [parts[i] + parts[i + 1] for i in range(0, len(parts), 2)]
        return parts[0]

    def regroup(call):
        for q in range(each):
            @pl.when(call * each + q < n_mem)
            def _():
                build(call * each + q + 1)

    def forward(call):
        for q in range(each):
            turn = call * each + q + 1

            @pl.when(turn < n_mem)
            def _():
                z_copy(turn).start()

    def turn_over(call):
        for q in range(each):
            turn = (call - 2) * each + q + 1

            @pl.when((turn >= 1) & (turn < n_mem))
            def _():
                z_copy(turn).wait()

            if cap % LANES == 0:

                @pl.when((turn >= 1) & (turn <= n_mem))
                def _():
                    at = pl.ds(pl.multiple_of((turn - 1) * cap, cap), cap)
                    zt_ref[:, at] = z_ref[at, :].T

    def all_sum(value, call, fills=True):
        value = exchange(
            value, call, near, me_near, near_peer, near_send, near_recv, ns_sem, nr_sem,
            functools.partial(regroup, call) if fills else None,
        )
        value = exchange(
            value, call, high, me_high, far_peer, far_send, far_recv, fs_sem, fr_sem,
            functools.partial(turn_over, call) if fills else None,
        )
        if fills:
            forward(call)
        return value

    def small_sum(value, call, between):
        value = jnp.broadcast_to(value, (1, LANES))
        if direct:
            value = exchange(
                value, call, n_grp * n_mem, me_all, any_peer, one_send, one_recv, os_sem, or_sem,
                between,
            )
            return value[:, 0:1]
        between()
        wide = jnp.broadcast_to(value, (lines, LANES))
        return all_sum(wide, NEWTON * CG_ITERS + call, False)[0:1, 0:1]

    def times_rows(vector, loading=False):
        row = jnp.concatenate([vector[i : i + 1, :] for i in range(lines)], axis=1)
        pair = pair_rows(row)
        parts = []
        for first in range(0, rows, 256):
            if loading:
                feat_loads[first // 256].wait()
            got = lax.dot_general(
                pair, feat[first : first + 256, :], NT, preferred_element_type=jnp.float32
            )
            parts.append(got[0:1] + got[1:2])
        return jnp.concatenate(parts, axis=1)

    def times_columns(row):
        pair = pair_rows(row)
        parts = []
        for first in range(0, width, 256):
            got = lax.dot_general(
                pair, feat[:, first : first + 256], NN, preferred_element_type=jnp.float32
            )
            got = got[0:1] + got[1:2]
            parts += [got[:, at : at + LANES] for at in range(0, 256, LANES)]
        return jnp.concatenate(parts, axis=0)

    def total(value):
        return jnp.sum(jnp.sum(value, axis=1, keepdims=True), axis=0, keepdims=True)

    scale = scale_ref[...]
    target = label_ref[...].astype(jnp.float32)

    score[...] = times_rows(scale * vec_w[...], True)

    def newton(step, carry):
        weights = vec_w[...]
        margin = score[...] + offset_ref[...]
        prob = 1.0 / (1.0 + jnp.exp(-margin))
        curv[...] = prob * (1.0 - prob)
        grad = times_columns(prob - target)

        @pl.when(step == 0)
        def _():
            for load in loads[4:]:
                load.wait()

        base = step * CG_ITERS
        resid = -(scale * all_sum(grad, base) + ridge_fixed * weights)
        vec_r[...] = resid
        vec_p[...] = resid
        vec_u[...] = jnp.zeros_like(resid)

        def cg(k, norm):
            direction = vec_p[...]
            along = times_rows(scale * direction)
            image = all_sum(times_columns(curv[...] * along), base + 1 + k)
            image = scale * image + ridge_fixed * direction
            size = norm / total(direction * image)
            vec_u[...] = vec_u[...] + size * direction
            score[...] = score[...] + size * along
            left = vec_r[...] - size * image
            vec_r[...] = left
            new_norm = total(left * left)
            vec_p[...] = left + new_norm / norm * direction
            return new_norm

        norm = lax.fori_loop(0, CG_ITERS - 1, cg, total(resid * resid))
        direction = vec_p[...]
        along = times_rows(scale * direction)

        def hand_out():
            @pl.when(step == NEWTON - 1)
            def _():
                send_rows(along)

        bend = small_sum(total(curv[...] * along * along), step, hand_out)
        size = norm / (bend + ridge_fixed * total(direction * direction))
        score[...] = score[...] + size * along
        vec_w[...] = weights + (vec_u[...] + size * direction)
        return size

    def send_rows(along):
        row_vals[...] = jnp.zeros_like(row_vals)
        row_vals[0:1, :] = score[...]
        row_vals[1:2, :] = along
        row_vals[2:3, :] = target
        row_vals[3:4, :] = lax.rem(member_ref[...], MEM_DEV).astype(jnp.float32) + 1.0
        parts = jnp.concatenate([p.astype(jnp.float32) for p in three_parts(row_vals[...])], axis=0)
        parts = jnp.concatenate([parts, jnp.zeros_like(parts[0:8])], axis=0).astype(jnp.bfloat16)
        for turn in range(1, n_mem + 1):
            first = pl.multiple_of(lax.rem(me_mem + turn, n_mem) * cap, cap)
            got = lax.dot_general(
                parts, pick[pl.ds(first, cap), :], NT, preferred_element_type=jnp.float32
            )
            got = got[0:8] + got[8:16] + got[16:24]
            if turn < n_mem:
                w_send[turn - 1] = got
                pltpu.make_async_remote_copy(
                    src_ref=w_send.at[turn - 1],
                    dst_ref=w_recv.at[turn - 1],
                    send_sem=ws_sem,
                    recv_sem=wr_sem,
                    device_id=peer(turn),
                    device_id_type=MESH_ID,
                ).start()
            else:
                w_recv[n_mem - 1] = got

    size = lax.fori_loop(0, NEWTON, newton, jnp.zeros((1, 1), jnp.float32))
    weight_ref[...] = vec_w[...]
    if cap % LANES:
        for first in range(0, slots, LANES):
            zt_ref[:, first : first + LANES] = z_ref[first : first + LANES, :].T
    others = w_recv.at[pl.ds(0, n_mem - 1)]
    pltpu.make_async_copy(others, others, wr_sem).wait()
    pltpu.make_async_copy(w_send, w_send, ws_sem).wait()
    arrived = jnp.concatenate([w_recv[t] for t in range(n_mem)], axis=1)
    prob = 1.0 / (1.0 + jnp.exp(-(arrived[0:1] + size * arrived[1:2])))
    coef = fit_members(
        z_ref, zt_ref, prob * (1.0 - prob), prob - arrived[2:3], arrived[3:4] - 1.0,
        gram, upper, lower,
    )
    coef_ref[...] = coef
    for turn in range(1, n_mem):
        pltpu.make_async_remote_copy(
            src_ref=coef_ref,
            dst_ref=c_recv.at[me_mem],
            send_sem=cs_sem,
            recv_sem=cr_sem,
            device_id=peer(turn),
            device_id_type=MESH_ID,
        ).start()
    c_recv[me_mem] = coef
    others = c_recv.at[pl.ds(0, n_mem - 1)]
    pltpu.make_async_copy(others, others, cr_sem).wait()
    pltpu.make_async_copy(others, others, cs_sem).wait()
    coefs = jnp.concatenate([c_recv[i] for i in range(n_mem)], axis=0)
    upper_part = coefs.astype(jnp.bfloat16)
    lower_part = (coefs - upper_part.astype(jnp.float32)).astype(jnp.bfloat16)
    got = lax.dot_general(
        jnp.concatenate([upper_part, lower_part], axis=0), re_ref[...], NT,
        preferred_element_type=jnp.float32,
    )
    members = n_mem * MEM_DEV
    at = lax.broadcasted_iota(jnp.int32, (members, rows), 0)
    own = at == lax.rem(member_ref[...], members)
    offsets_ref[...] = jnp.sum(
        jnp.where(own, got[0:members] + got[members:], 0.0), axis=0, keepdims=True
    )


def hand_over(*refs):
    for source, target in zip(refs[:3], refs[3:]):
        target[...] = source[...]


def on_device(n_grp, n_mem, features, re_features, member_id, slot, labels, offsets, feature_scale, w_start):
    rows, width = features.shape
    inner = re_features.shape[1]
    lines = width // LANES
    slots = 2 * rows
    cap = slots // n_mem
    near, high = 2 * n_grp, n_mem // 2
    direct = n_grp * n_mem <= 32
    calls = NEWTON * CG_ITERS if direct else NEWTON * (CG_ITERS + 1)
    every = n_grp * n_mem if direct else 2
    f32, bf16, i32 = jnp.float32, jnp.bfloat16, jnp.int32
    held = pltpu.VMEM((lines, LANES), f32)
    dma = pltpu.SemaphoreType.DMA
    whole = pl.BlockSpec(memory_space=pltpu.VMEM)
    weights, member_coef, row_offsets = pl.pallas_call(
        functools.partial(window_kernel, n_grp, n_mem),
        out_shape=(
            jax.ShapeDtypeStruct((lines, LANES), f32),
            jax.ShapeDtypeStruct((MEM_DEV, inner), f32),
            jax.ShapeDtypeStruct((1, rows), f32),
        ),
        in_specs=[pl.BlockSpec(memory_space=pl.ANY)] * 8,
        out_specs=(whole,) * 3,
        scratch_shapes=[
            pltpu.VMEM((rows, width), bf16),
            pltpu.VMEM((rows, inner), bf16),
            pltpu.VMEM((1, rows), i32),
            pltpu.VMEM((1, rows), i32),
            pltpu.VMEM((1, rows), i32),
            pltpu.VMEM((1, rows), f32),
            held, held, held, held, held,
            pltpu.VMEM((1, rows), f32),
            pltpu.VMEM((1, rows), f32),
            pltpu.VMEM((calls, lines, LANES), f32),
            pltpu.VMEM((calls, near, lines, LANES), f32),
            pltpu.VMEM((calls, lines, LANES), f32),
            pltpu.VMEM((calls, high, lines, LANES), f32),
            pltpu.VMEM((NEWTON, 1, LANES), f32),
            pltpu.VMEM((NEWTON, every, 1, LANES), f32),
            pltpu.VMEM((slots, rows), bf16),
            pltpu.VMEM((n_mem - 1, cap, inner), bf16),
            pltpu.VMEM((slots, inner), bf16),
            pltpu.VMEM((inner, slots), bf16),
            pltpu.VMEM((n_mem - 1, 8, cap), f32),
            pltpu.VMEM((n_mem, 8, cap), f32),
            pltpu.VMEM((n_mem, MEM_DEV, inner), f32),
            pltpu.VMEM((MEM_DEV, inner, inner), f32),
            pltpu.VMEM((inner, slots), bf16),
            pltpu.VMEM((inner, slots), bf16),
            pltpu.VMEM((8, rows), f32),
            dma((7,)),
            dma((rows // 256,)),
            dma((calls,)),
            dma((calls,)),
            dma((calls,)),
            dma((calls,)),
            dma((NEWTON,)),
            dma((NEWTON,)),
            dma((n_mem - 1,)),
            dma((n_mem - 1,)),
            dma, dma, dma, dma,
        ],
        compiler_params=pltpu.CompilerParams(
            collective_id=0, has_side_effects=True, vmem_limit_bytes=60 << 20
        ),
        name="window",
    )(
        features,
        re_features,
        member_id.reshape(1, rows),
        slot.reshape(1, rows),
        labels.reshape(1, rows),
        offsets.reshape(1, rows),
        feature_scale.reshape(lines, LANES),
        w_start.reshape(lines, LANES),
    )
    weights, member_coef, row_offsets = pl.pallas_call(
        hand_over,
        out_shape=tuple(
            jax.ShapeDtypeStruct(x.shape, x.dtype) for x in (weights, member_coef, row_offsets)
        ),
        in_specs=[whole] * 3,
        out_specs=(whole,) * 3,
        name="hand_over",
    )(weights, member_coef, row_offsets)
    return (weights.reshape(-1), member_coef, row_offsets.reshape(-1))


def solution(mesh):
    placed = (
        P(("grp", "mem"), None),
        P(("grp", "mem"), None),
        P(("grp", "mem")),
        P(("grp", "mem")),
        P(("grp", "mem")),
        P(("grp", "mem")),
        P(),
        P(),
    )
    return jax.shard_map(
        functools.partial(on_device, mesh.shape["grp"], mesh.shape["mem"]),
        mesh=mesh,
        in_specs=placed,
        out_specs=(P(), P(("grp", "mem"), None), P(("grp", "mem"))),
        check_vma=False,
    )
```

```python
import functools

import jax
import jax.numpy as jnp
from jax import lax
from jax.experimental import pallas as pl
from jax.experimental.pallas import tpu as pltpu
from jax.sharding import PartitionSpec as P

MEM_DEV = 8
NEWTON = 2
CG_ITERS = 3
LANES = 128
BLOCK = 32
PARTS = 2

ridge_fixed = 1.0
ridge_member = 1.0
MESH_ID = pl.DeviceIdType.MESH
NT = (((1,), (1,)), ((), ()))
NN = (((1,), (0,)), ((), ()))
TN = (((0,), (0,)), ((), ()))


def three_parts(value):
    first = value.astype(jnp.bfloat16)
    rest = value - first.astype(jnp.float32)
    second = rest.astype(jnp.bfloat16)
    third = (rest - second.astype(jnp.float32)).astype(jnp.bfloat16)
    return first, second, third


def pair_rows(row):
    at = lax.broadcasted_iota(jnp.int32, (16, row.shape[1]), 0)
    both = jnp.zeros((16, row.shape[1]), jnp.float32)
    for i, part in enumerate(three_parts(row)):
        both = jnp.where(at == i, part.astype(jnp.float32), both)
    return both.astype(jnp.bfloat16)


def tree_sum(parts):
    while len(parts) > 1:
        parts = [parts[i] + parts[i + 1] for i in range(0, len(parts), 2)]
    return parts[0]


def split_six(value, axis, left):
    first, second, third = three_parts(value)
    if left:
        return jnp.concatenate([first, first, second, second, first, third], axis=axis)
    return jnp.concatenate([first, second, first, second, third, first], axis=axis)


def invert_blocks(blocks):
    lane = lax.broadcasted_iota(jnp.int32, (BLOCK, LANES), 1)
    sub = lax.broadcasted_iota(jnp.int32, (BLOCK, LANES), 0)
    base = lane // BLOCK * BLOCK
    place = lane % BLOCK

    def column(value, k):
        return jnp.take_along_axis(value, base + k, axis=1)

    blocks = [(value, column(value, 0), column(value, 1)) for value in blocks]
    for k in range(0, BLOCK, 2):
        one, two = place == k, place == k + 1
        at_one, at_two = one[0:1, :], two[0:1, :]
        new = []
        for value, left, right in blocks:
            ahead = [column(value, k + 2), column(value, k + 3)] if k + 2 < BLOCK else []
            a, b = left[k : k + 1, :], right[k : k + 1, :]
            c, d = left[k + 1 : k + 2, :], right[k + 1 : k + 2, :]
            inverse = 1.0 / (a * d - b * c)
            a, b, c, d = d * inverse, -b * inverse, -c * inverse, a * inverse

            def update(value, first, second):
                value = value - left * first - right * second
                return jnp.where(sub == k, first, jnp.where(sub == k + 1, second, value))

            following = []
            for col in ahead:
                top, low = col[k : k + 1, :], col[k + 1 : k + 2, :]
                following.append(update(col, a * top + b * low, c * top + d * low))
            top, low = value[k : k + 1, :], value[k + 1 : k + 2, :]
            first = jnp.where(at_one, a, jnp.where(at_two, b, a * top + b * low))
            second = jnp.where(at_one, c, jnp.where(at_two, d, c * top + d * low))
            value = update(jnp.where(one | two, 0.0, value), first, second)
            new.append((value, *(following or (left, right))))
        blocks = new
        yield [value for value, _, _ in blocks]


def fit_members(z_ref, zt_ref, curv_row, resid_row, local, gram, upper, lower):
    width = z_ref.shape[1]
    slots = z_ref.shape[0]
    count = MEM_DEV
    per = LANES // BLOCK
    blocks = width // BLOCK
    weighted = zt_ref[...].astype(jnp.float32) * curv_row
    first = weighted.astype(jnp.bfloat16)
    upper[...] = first
    lower[...] = (weighted - first.astype(jnp.float32)).astype(jnp.bfloat16)
    eye = (
        lax.broadcasted_iota(jnp.int32, (width, width), 0)
        == lax.broadcasted_iota(jnp.int32, (width, width), 1)
    ).astype(jnp.float32)

    @pl.loop(0, count)
    def _(m):
        mask = jnp.where(local == m.astype(jnp.float32), 1.0, 0.0).astype(jnp.bfloat16)
        total = lax.dot_general(
            upper[...] * mask, z_ref[...], NN, preferred_element_type=jnp.float32
        ) + lax.dot_general(
            lower[...] * mask, z_ref[...], NN, preferred_element_type=jnp.float32
        )
        gram[m] = total + ridge_member * eye

    member = lax.broadcasted_iota(jnp.int32, (count, slots), 0).astype(jnp.float32)
    masked = jnp.where(member == local, resid_row, 0.0)
    high = masked.astype(jnp.bfloat16)
    low = (masked - high.astype(jnp.float32)).astype(jnp.bfloat16)
    goal = lax.dot_general(
        high, z_ref[...], NN, preferred_element_type=jnp.float32
    ) + lax.dot_general(low, z_ref[...], NN, preferred_element_type=jnp.float32)

    place = lax.broadcasted_iota(jnp.int32, (1, width), 1)
    turn = lax.broadcasted_iota(jnp.int32, (count, width), 0)
    lane = lax.broadcasted_iota(jnp.int32, (BLOCK, LANES), 1)
    unit = lax.broadcasted_iota(jnp.int32, (BLOCK, width), 1)
    unit = unit - lax.broadcasted_iota(jnp.int32, (BLOCK, width), 0)
    later = []

    def trailing(m, first, inside, left, right):
        update = lax.dot_general(left, right, TN, preferred_element_type=jnp.float32)
        gram[m, first:width, :] = jnp.where(inside, 0.0, gram[m, first:width, :]) - update

    rows_now = [gram[m, 0:BLOCK, :] for m in range(count)]
    for b in range(blocks):
        lo, hi = b * BLOCK, (b + 1) * BLOCK
        packed = [
            jnp.concatenate([rows_now[m][:, lo:hi] for m in range(at, at + per)], axis=1)
            for at in range(0, count, per)
        ]
        for step, packed in enumerate(invert_blocks(packed)):
            if later and step % 2 == 1:
                later.pop(0)()
        while later:
            later.pop(0)()
        inside = (place >= lo) & (place < hi)
        panels = []
        for index, value in enumerate(packed):
            left = jnp.concatenate(
                [jnp.where(lane // BLOCK == i, value, 0.0) for i in range(per)], axis=0
            )
            right = jnp.concatenate(
                [
                    jnp.where(inside, jnp.where(unit == lo, -1.0, 0.0), rows_now[index * per + i])
                    for i in range(per)
                ],
                axis=0,
            )
            got = lax.dot_general(
                split_six(left, 1, True), split_six(right, 0, False), NN,
                preferred_element_type=jnp.float32,
            )
            panels += [got[i * BLOCK : (i + 1) * BLOCK, :] for i in range(per)]
        heads = split_six(goal[:, lo:hi], 1, True)
        goal = jnp.where(inside, 0.0, goal)
        following = []
        for m in range(count):
            right = split_six(panels[m], 0, False)
            if hi < width:
                left = split_six(rows_now[m][:, hi:], 0, True)
                update = lax.dot_general(
                    left[:, 0:BLOCK], right, TN, preferred_element_type=jnp.float32
                )
                following.append(jnp.where(inside, 0.0, gram[m, hi : hi + BLOCK, :]) - update)
                if hi + BLOCK < width:
                    later.append(
                        functools.partial(
                            trailing, m, hi + BLOCK, inside, left[:, BLOCK:], right
                        )
                    )
            update = lax.dot_general(heads, right, NN, preferred_element_type=jnp.float32)
            goal = goal - jnp.where(turn == m, update, 0.0)
        rows_now = following
    return -goal


def window_kernel(
    n_grp, n_mem,
    feat_hbm, re_hbm, member_hbm, slot_hbm, label_hbm, offset_hbm, scale_hbm, start_hbm,
    weight_ref, coef_ref, offsets_ref,
    feat, feat_t, re_ref, member_ref, slot_ref, label_ref, offset_ref, scale_ref, vec_w,
    vec_u, vec_r, vec_p, curv, score, along_ref, rest_ref, near_send, near_recv, far_send, far_recv, one_send, one_recv,
    pick, z_send, z_ref, zt_ref, w_send, w_recv, c_recv, gram, upper, lower, row_vals,
    load_sem, feat_sem, ns_sem, nr_sem, fs_sem, fr_sem, os_sem, or_sem, zs_sem, zr_sem, ws_sem, wr_sem, cs_sem, cr_sem,
):
    rows, width = feat.shape
    lines = width // LANES
    half = lines // PARTS
    slots = z_ref.shape[0]
    cap = slots // n_mem
    each = (n_mem - 1) // (NEWTON * CG_ITERS)
    early = n_mem - each * NEWTON * CG_ITERS
    direct = n_grp * n_mem <= 32
    me_grp = lax.axis_index("grp")
    me_mem = lax.axis_index("mem")

    loads = [
        pltpu.make_async_copy(source, target, load_sem.at[i])
        for i, (source, target) in enumerate(
            (
                (scale_hbm, scale_ref), (start_hbm, vec_w), (offset_hbm, offset_ref),
                (label_hbm, label_ref), (slot_hbm, slot_ref), (member_hbm, member_ref),
                (re_hbm, re_ref),
            )
        )
    ]
    feat_loads = [
        pltpu.make_async_copy(
            feat_hbm.at[pl.ds(first, 256)], feat.at[pl.ds(first, 256)], feat_sem.at[first // 256]
        )
        for first in range(0, rows, 256)
    ]
    for load in loads + feat_loads:
        load.start()

    low = 2
    high = n_mem // low
    near = n_grp * low
    me_low = lax.rem(me_mem, low)
    me_high = me_mem // low
    me_near = me_grp * low + me_low

    def near_peer(turn):
        other = lax.rem(me_near + turn, near)
        return (other // low, me_high * low + lax.rem(other, low))

    def far_peer(turn):
        return (me_grp, lax.rem(me_high + turn, high) * low + me_low)

    me_all = me_grp * n_mem + me_mem

    def any_peer(turn):
        other = lax.rem(me_all + turn, n_grp * n_mem)
        return (other // n_mem, lax.rem(other, n_mem))

    barrier = pltpu.get_barrier_semaphore()
    if direct:
        for turn in range(1, n_grp * n_mem):
            pl.semaphore_signal(barrier, inc=1, device_id=any_peer(turn), device_id_type=MESH_ID)
        greeted = n_grp * n_mem - 1
    else:
        for turn in range(1, n_mem):
            pl.semaphore_signal(
                barrier, inc=1, device_id=(me_grp, lax.rem(me_mem + turn, n_mem)), device_id_type=MESH_ID
            )
        for turn in range(1, near):
            pl.semaphore_signal(barrier, inc=1, device_id=near_peer(turn), device_id_type=MESH_ID)
        greeted = n_mem - 1 + near - 1

    def peer(turn):
        return (me_grp, lax.rem(me_mem + turn, n_mem))

    def z_copy(turn):
        return pltpu.make_async_remote_copy(
            src_ref=z_send.at[turn - 1],
            dst_ref=z_ref.at[pl.ds(pl.multiple_of((turn - 1) * cap, cap), cap)],
            send_sem=zs_sem.at[turn - 1],
            recv_sem=zr_sem.at[turn - 1],
            device_id=peer(turn),
            device_id_type=MESH_ID,
        )

    def build(turn):
        first = pl.multiple_of(lax.rem(me_mem + turn, n_mem) * cap, cap)
        at = lax.broadcasted_iota(jnp.int32, (cap, rows), 0) + first
        chosen = jnp.where(at == slot_ref[...], 1.0, 0.0).astype(jnp.bfloat16)
        pick[pl.ds(first, cap), :] = chosen
        block = lax.dot_general(chosen, re_ref[...], NN, preferred_element_type=jnp.float32)
        block = block.astype(jnp.bfloat16)

        @pl.when(turn < n_mem)
        def _():
            z_send[turn - 1] = block

        @pl.when(turn == n_mem)
        def _():
            z_ref[(n_mem - 1) * cap :, :] = block

    def begin(value, call, part, size, me, peer_of, source, slots_of, sends, recvs):
        at = pl.ds(part * half, half)
        source[call, at] = value
        for turn in range(1, size):
            pltpu.make_async_remote_copy(
                src_ref=source.at[call, at],
                dst_ref=slots_of.at[call, me, at],
                send_sem=sends.at[call, part],
                recv_sem=recvs.at[call, part],
                device_id=peer_of(turn),
                device_id_type=MESH_ID,
            ).start()
        slots_of[call, me, at] = value

    def finish(call, part, size, slots_of, sends, recvs):
        at = pl.ds(part * half, half)
        others = slots_of.at[call, pl.ds(0, size - 1), at]
        pltpu.make_async_copy(others, others, recvs.at[call, part]).wait()
        pltpu.make_async_copy(others, others, sends.at[call, part]).wait()
        return tree_sum([slots_of[call, i, at] for i in range(size)])

    def begin_near(value, call, part):
        begin(value, call, part, near, me_near, near_peer, near_send, near_recv, ns_sem, nr_sem)

    def finish_near(call, part):
        return finish(call, part, near, near_recv, ns_sem, nr_sem)

    def begin_far(value, call, part):
        begin(value, call, part, high, me_high, far_peer, far_send, far_recv, fs_sem, fr_sem)

    def finish_far(call, part):
        return finish(call, part, high, far_recv, fs_sem, fr_sem)

    def regroup(call):
        for q in range(each):
            build(early + call * each + q + 1)

    def forward(call):
        for q in range(each):
            turn = early + call * each + q + 1

            @pl.when(turn < n_mem)
            def _():
                z_copy(turn).start()

    def settle(turn):
        @pl.when(turn < n_mem)
        def _():
            z_copy(turn).wait()

        if cap % LANES == 0:
            at = pl.ds(pl.multiple_of((turn - 1) * cap, cap), cap)
            zt_ref[:, at] = z_ref[at, :].T

    def turn_over(call):
        for q in range(each):
            settle(call * each + q + 1)

        @pl.when(call == NEWTON * CG_ITERS - 1)
        def _():
            for q in range(early):
                settle((call + 1) * each + q + 1)

    def reduce_columns(row, call):
        pair = pair_rows(row)
        for part in range(PARTS):
            begin_near(times_columns(pair, part), call, part)
        @pl.when(call == 0)
        def _():
            transpose_features()

        regroup(call)
        for part in range(PARTS):
            begin_far(finish_near(call, part), call, part)
        turn_over(call)
        sums, image = [], None
        for part in range(PARTS):
            value = scale[part * half : (part + 1) * half] * finish_far(call, part)
            if part == PARTS - 1:
                forward(call)
            got = times_rows(value, part)
            image = got if image is None else image + got
            sums.append(value)
        return jnp.concatenate(sums, axis=0), image

    def small_sum(value, call, between):
        if direct:
            value = jnp.broadcast_to(value, (1, LANES))
            one_send[call] = value
            for turn in range(1, n_grp * n_mem):
                pltpu.make_async_remote_copy(
                    src_ref=one_send.at[call],
                    dst_ref=one_recv.at[call, me_all],
                    send_sem=os_sem.at[call],
                    recv_sem=or_sem.at[call],
                    device_id=any_peer(turn),
                    device_id_type=MESH_ID,
                ).start()
            one_recv[call, me_all] = value
            between()
            others = one_recv.at[call, pl.ds(0, n_grp * n_mem - 1)]
            pltpu.make_async_copy(others, others, or_sem.at[call]).wait()
            pltpu.make_async_copy(others, others, os_sem.at[call]).wait()
            return tree_sum([one_recv[call, i] for i in range(n_grp * n_mem)])[:, 0:1]
        between()
        call = NEWTON * CG_ITERS + call
        begin_near(jnp.broadcast_to(value, (half, LANES)), call, 0)
        begin_far(finish_near(call, 0), call, 0)
        return finish_far(call, 0)[0:1, 0:1]

    def first_rows(vector):
        pair = pair_rows(jnp.concatenate([vector[i : i + 1, :] for i in range(lines)], axis=1))
        parts = []
        for first in range(0, rows, 256):
            feat_loads[first // 256].wait()
            got = lax.dot_general(
                pair, feat[first : first + 256, :], NT, preferred_element_type=jnp.float32
            )
            parts.append(got[0:1] + got[1:2] + got[2:3])
        return jnp.concatenate(parts, axis=1)

    def transpose_features():
        @pl.loop(0, rows // 256)
        def _(r):
            at = pl.ds(pl.multiple_of(r * 256, 256), 256)
            for first in range(0, width, 256):
                feat_t[first : first + 256, at] = feat[at, first : first + 256].T

    def times_rows(value, part):
        vector = scale[part * half : (part + 1) * half] * value
        pair = pair_rows(jnp.concatenate([vector[i : i + 1, :] for i in range(half)], axis=1))
        at = slice(part * half * LANES, (part + 1) * half * LANES)
        parts = []
        for first in range(0, rows, 256):
            got = lax.dot_general(
                pair, feat_t[at, first : first + 256], NN, preferred_element_type=jnp.float32
            )
            parts.append(got[0:1] + got[1:2] + got[2:3])
        return jnp.concatenate(parts, axis=1)

    def times_columns(pair, part):
        parts = []
        for first in range(part * half * LANES, (part + 1) * half * LANES, 256):
            got = lax.dot_general(
                pair, feat[:, first : first + 256], NN, preferred_element_type=jnp.float32
            )
            got = got[0:1] + got[1:2] + got[2:3]
            parts += [got[:, at : at + LANES] for at in range(0, 256, LANES)]
        return jnp.concatenate(parts, axis=0)

    def total(value):
        return jnp.sum(jnp.sum(value, axis=1, keepdims=True), axis=0, keepdims=True)

    for load in loads:
        load.wait()
    scale = scale_ref[...]
    target = label_ref[...].astype(jnp.float32)

    for turn in range(1, early + 1):
        build(turn)
    pl.semaphore_wait(barrier, greeted)
    for turn in range(1, early + 1):
        z_copy(turn).start()
    score[...] = first_rows(scale * vec_w[...])

    def newton(step, carry):
        weights = vec_w[...]
        margin = score[...] + offset_ref[...]
        prob = 1.0 / (1.0 + jnp.exp(-margin))
        curv[...] = prob * (1.0 - prob)

        base = step * CG_ITERS
        summed, along = reduce_columns(prob - target, base)
        resid = -(summed + ridge_fixed * weights)
        along = -(along + ridge_fixed * score[...])
        vec_r[...] = resid
        vec_p[...] = resid
        vec_u[...] = jnp.zeros_like(resid)
        rest_ref[...] = along
        along_ref[...] = along

        def cg(k, norm):
            direction = vec_p[...]
            along = along_ref[...]
            image, seen = reduce_columns(curv[...] * along, base + 1 + k)
            image = image + ridge_fixed * direction
            size = norm / total(direction * image)
            vec_u[...] = vec_u[...] + size * direction
            score[...] = score[...] + size * along
            left = vec_r[...] - size * image
            vec_r[...] = left
            rest = rest_ref[...] - size * (seen + ridge_fixed * along)
            rest_ref[...] = rest
            new_norm = total(left * left)
            turned = new_norm / norm
            vec_p[...] = left + turned * direction
            along_ref[...] = rest + turned * along
            return new_norm

        norm = lax.fori_loop(0, CG_ITERS - 1, cg, total(resid * resid))
        direction = vec_p[...]
        along = along_ref[...]

        def hand_out():
            @pl.when(step == NEWTON - 1)
            def _():
                send_rows(along)

        bend = small_sum(total(curv[...] * along * along), step, hand_out)
        size = norm / (bend + ridge_fixed * total(direction * direction))
        score[...] = score[...] + size * along
        vec_w[...] = weights + (vec_u[...] + size * direction)
        return size

    def send_rows(along):
        row_vals[...] = jnp.zeros_like(row_vals)
        row_vals[0:1, :] = score[...]
        row_vals[1:2, :] = along
        row_vals[2:3, :] = target
        row_vals[3:4, :] = lax.rem(member_ref[...], MEM_DEV).astype(jnp.float32) + 1.0
        parts = jnp.concatenate([p.astype(jnp.float32) for p in three_parts(row_vals[...])], axis=0)
        parts = jnp.concatenate([parts, jnp.zeros_like(parts[0:8])], axis=0).astype(jnp.bfloat16)
        for turn in range(1, n_mem + 1):
            first = pl.multiple_of(lax.rem(me_mem + turn, n_mem) * cap, cap)
            got = lax.dot_general(
                parts, pick[pl.ds(first, cap), :], NT, preferred_element_type=jnp.float32
            )
            got = got[0:8] + got[8:16] + got[16:24]
            if turn < n_mem:
                w_send[turn - 1] = got
                pltpu.make_async_remote_copy(
                    src_ref=w_send.at[turn - 1],
                    dst_ref=w_recv.at[turn - 1],
                    send_sem=ws_sem,
                    recv_sem=wr_sem,
                    device_id=peer(turn),
                    device_id_type=MESH_ID,
                ).start()
            else:
                w_recv[n_mem - 1] = got

    size = lax.fori_loop(0, NEWTON, newton, jnp.zeros((1, 1), jnp.float32))
    weight_ref[...] = vec_w[...]
    if cap % LANES:
        for first in range(0, slots, LANES):
            zt_ref[:, first : first + LANES] = z_ref[first : first + LANES, :].T
    others = w_recv.at[pl.ds(0, n_mem - 1)]
    pltpu.make_async_copy(others, others, wr_sem).wait()
    pltpu.make_async_copy(w_send, w_send, ws_sem).wait()
    arrived = jnp.concatenate([w_recv[t] for t in range(n_mem)], axis=1)
    prob = 1.0 / (1.0 + jnp.exp(-(arrived[0:1] + size * arrived[1:2])))
    coef = fit_members(
        z_ref, zt_ref, prob * (1.0 - prob), prob - arrived[2:3], arrived[3:4] - 1.0,
        gram, upper, lower,
    )
    coef_ref[...] = coef
    for turn in range(1, n_mem):
        pltpu.make_async_remote_copy(
            src_ref=coef_ref,
            dst_ref=c_recv.at[me_mem],
            send_sem=cs_sem,
            recv_sem=cr_sem,
            device_id=peer(turn),
            device_id_type=MESH_ID,
        ).start()
    c_recv[me_mem] = coef
    others = c_recv.at[pl.ds(0, n_mem - 1)]
    pltpu.make_async_copy(others, others, cr_sem).wait()
    pltpu.make_async_copy(others, others, cs_sem).wait()
    coefs = jnp.concatenate([c_recv[i] for i in range(n_mem)], axis=0)
    upper_part = coefs.astype(jnp.bfloat16)
    lower_part = (coefs - upper_part.astype(jnp.float32)).astype(jnp.bfloat16)
    got = lax.dot_general(
        jnp.concatenate([upper_part, lower_part], axis=0), re_ref[...], NT,
        preferred_element_type=jnp.float32,
    )
    members = n_mem * MEM_DEV
    at = lax.broadcasted_iota(jnp.int32, (members, rows), 0)
    own = at == lax.rem(member_ref[...], members)
    offsets_ref[...] = jnp.sum(
        jnp.where(own, got[0:members] + got[members:], 0.0), axis=0, keepdims=True
    )


def hand_over(*refs):
    for source, target in zip(refs[:3], refs[3:]):
        target[...] = source[...]


def on_device(n_grp, n_mem, features, re_features, member_id, slot, labels, offsets, feature_scale, w_start):
    rows, width = features.shape
    inner = re_features.shape[1]
    lines = width // LANES
    slots = 2 * rows
    cap = slots // n_mem
    near, high = 2 * n_grp, n_mem // 2
    direct = n_grp * n_mem <= 32
    calls = NEWTON * CG_ITERS if direct else NEWTON * (CG_ITERS + 1)
    every = n_grp * n_mem if direct else 2
    f32, bf16, i32 = jnp.float32, jnp.bfloat16, jnp.int32
    held = pltpu.VMEM((lines, LANES), f32)
    dma = pltpu.SemaphoreType.DMA
    whole = pl.BlockSpec(memory_space=pltpu.VMEM)
    weights, member_coef, row_offsets = pl.pallas_call(
        functools.partial(window_kernel, n_grp, n_mem),
        out_shape=(
            jax.ShapeDtypeStruct((lines, LANES), f32),
            jax.ShapeDtypeStruct((MEM_DEV, inner), f32),
            jax.ShapeDtypeStruct((1, rows), f32),
        ),
        in_specs=[pl.BlockSpec(memory_space=pl.ANY)] * 8,
        out_specs=(whole,) * 3,
        scratch_shapes=[
            pltpu.VMEM((rows, width), bf16),
            pltpu.VMEM((width, rows), bf16),
            pltpu.VMEM((rows, inner), bf16),
            pltpu.VMEM((1, rows), i32),
            pltpu.VMEM((1, rows), i32),
            pltpu.VMEM((1, rows), i32),
            pltpu.VMEM((1, rows), f32),
            held, held, held, held, held,
            pltpu.VMEM((1, rows), f32),
            pltpu.VMEM((1, rows), f32),
            pltpu.VMEM((1, rows), f32),
            pltpu.VMEM((1, rows), f32),
            pltpu.VMEM((calls, lines, LANES), f32),
            pltpu.VMEM((calls, near, lines, LANES), f32),
            pltpu.VMEM((calls, lines, LANES), f32),
            pltpu.VMEM((calls, high, lines, LANES), f32),
            pltpu.VMEM((NEWTON, 1, LANES), f32),
            pltpu.VMEM((NEWTON, every, 1, LANES), f32),
            pltpu.VMEM((slots, rows), bf16),
            pltpu.VMEM((n_mem - 1, cap, inner), bf16),
            pltpu.VMEM((slots, inner), bf16),
            pltpu.VMEM((inner, slots), bf16),
            pltpu.VMEM((n_mem - 1, 8, cap), f32),
            pltpu.VMEM((n_mem, 8, cap), f32),
            pltpu.VMEM((n_mem, MEM_DEV, inner), f32),
            pltpu.VMEM((MEM_DEV, inner, inner), f32),
            pltpu.VMEM((inner, slots), bf16),
            pltpu.VMEM((inner, slots), bf16),
            pltpu.VMEM((8, rows), f32),
            dma((7,)),
            dma((rows // 256,)),
            dma((calls, PARTS)),
            dma((calls, PARTS)),
            dma((calls, PARTS)),
            dma((calls, PARTS)),
            dma((NEWTON,)),
            dma((NEWTON,)),
            dma((n_mem - 1,)),
            dma((n_mem - 1,)),
            dma, dma, dma, dma,
        ],
        compiler_params=pltpu.CompilerParams(
            collective_id=0, has_side_effects=True, vmem_limit_bytes=60 << 20
        ),
        name="window",
    )(
        features,
        re_features,
        member_id.reshape(1, rows),
        slot.reshape(1, rows),
        labels.reshape(1, rows),
        offsets.reshape(1, rows),
        feature_scale.reshape(lines, LANES),
        w_start.reshape(lines, LANES),
    )
    weights, member_coef, row_offsets = pl.pallas_call(
        hand_over,
        out_shape=tuple(
            jax.ShapeDtypeStruct(x.shape, x.dtype) for x in (weights, member_coef, row_offsets)
        ),
        in_specs=[whole] * 3,
        out_specs=(whole,) * 3,
        name="hand_over",
    )(weights, member_coef, row_offsets)
    return (weights.reshape(-1), member_coef, row_offsets.reshape(-1))


def solution(mesh):
    placed = (
        P(("grp", "mem"), None),
        P(("grp", "mem"), None),
        P(("grp", "mem")),
        P(("grp", "mem")),
        P(("grp", "mem")),
        P(("grp", "mem")),
        P(),
        P(),
    )
    return jax.shard_map(
        functools.partial(on_device, mesh.shape["grp"], mesh.shape["mem"]),
        mesh=mesh,
        in_specs=placed,
        out_specs=(P(), P(("grp", "mem"), None), P(("grp", "mem"))),
        check_vma=False,
    )
```

```python
import functools

import jax
import jax.numpy as jnp
from jax import lax
from jax.experimental import pallas as pl
from jax.experimental.pallas import tpu as pltpu
from jax.sharding import PartitionSpec as P

MEM_DEV = 8
NEWTON = 2
CG_ITERS = 3
LANES = 128
BLOCK = 32
PARTS = 2
ORDER = (4, 3, 5, 2, 7, 6, 1, 8)

ridge_fixed = 1.0
ridge_member = 1.0
MESH_ID = pl.DeviceIdType.MESH
NT = (((1,), (1,)), ((), ()))
NN = (((1,), (0,)), ((), ()))
TN = (((0,), (0,)), ((), ()))


def three_parts(value):
    first = value.astype(jnp.bfloat16)
    rest = value - first.astype(jnp.float32)
    second = rest.astype(jnp.bfloat16)
    third = (rest - second.astype(jnp.float32)).astype(jnp.bfloat16)
    return first, second, third


def pair_rows(row):
    at = lax.broadcasted_iota(jnp.int32, (16, row.shape[1]), 0)
    both = jnp.zeros((16, row.shape[1]), jnp.float32)
    for i, part in enumerate(three_parts(row)):
        both = jnp.where(at == i, part.astype(jnp.float32), both)
    return both.astype(jnp.bfloat16)


def tree_sum(parts):
    while len(parts) > 1:
        parts = [parts[i] + parts[i + 1] for i in range(0, len(parts), 2)]
    return parts[0]


def split_six(value, axis, left):
    first, second, third = three_parts(value)
    if left:
        return jnp.concatenate([first, first, second, second, first, third], axis=axis)
    return jnp.concatenate([first, second, first, second, third, first], axis=axis)


def invert_blocks(blocks):
    lane = lax.broadcasted_iota(jnp.int32, (BLOCK, LANES), 1)
    sub = lax.broadcasted_iota(jnp.int32, (BLOCK, LANES), 0)
    base = lane // BLOCK * BLOCK
    place = lane % BLOCK

    def column(value, k):
        return jnp.take_along_axis(value, base + k, axis=1)

    def spread(value, k):
        return jnp.broadcast_to(value[k : k + 1, :], (8, LANES))

    def tall(value):
        return jnp.concatenate([value] * (BLOCK // 8), axis=0)

    def start(value):
        left, right = column(value, 0), column(value, 1)
        corner = [spread(col, k) for k in (0, 1) for col in (left, right)]
        return value, left, right, corner

    blocks = [start(value) for value in blocks]
    for k in range(0, BLOCK, 2):
        one, two = place == k, place == k + 1
        at_one, at_two = one[0:8, :], two[0:8, :]
        more = k + 2 < BLOCK
        new = []
        for value, left, right, (a, b, c, d) in blocks:
            ahead = [column(value, k + 2), column(value, k + 3)] if more else []
            inverse = 1.0 / (a * d - b * c)
            a, b, c, d = d * inverse, -b * inverse, -c * inverse, a * inverse

            def update(value, first, second):
                first, second = tall(first), tall(second)
                value = value - left * first - right * second
                return jnp.where(sub == k, first, jnp.where(sub == k + 1, second, value))

            firsts = [a * spread(col, k) + b * spread(col, k + 1) for col in ahead]
            seconds = [c * spread(col, k) + d * spread(col, k + 1) for col in ahead]
            corner = [
                spread(col, at) - spread(left, at) * first - spread(right, at) * second
                for at in ((k + 2, k + 3) if more else ())
                for col, first, second in zip(ahead, firsts, seconds)
            ]
            following = [
                update(col, first, second) for col, first, second in zip(ahead, firsts, seconds)
            ]
            top, low = spread(value, k), spread(value, k + 1)
            first = jnp.where(at_one, a, jnp.where(at_two, b, a * top + b * low))
            second = jnp.where(at_one, c, jnp.where(at_two, d, c * top + d * low))
            value = update(jnp.where(one | two, 0.0, value), first, second)
            new.append((value, *(following or (left, right)), corner or (a, b, c, d)))
        blocks = new
        yield [value for value, *_ in blocks]


def fit_members(z_ref, zt_ref, curv_row, resid_row, local, gram, upper, lower, mixed):
    width = z_ref.shape[1]
    slots = z_ref.shape[0]
    count = MEM_DEV
    per = LANES // BLOCK
    blocks = width // BLOCK
    side = width // 2
    column = jnp.broadcast_to(curv_row, (LANES, slots)).T
    column = jnp.concatenate([column] * (width // LANES), axis=1)
    weighted = z_ref[...].astype(jnp.float32) * column
    first = weighted.astype(jnp.bfloat16)
    second = (weighted - first.astype(jnp.float32)).astype(jnp.bfloat16)
    upper[...] = first
    lower[...] = second
    mixed[:, 0:side] = first[:, side:]
    mixed[:, side:] = second[:, side:]
    eye = (
        lax.broadcasted_iota(jnp.int32, (width, width), 0)
        == lax.broadcasted_iota(jnp.int32, (width, width), 1)
    ).astype(jnp.float32)

    @pl.loop(0, count, step=2)
    def _(m):
        masks = [
            jnp.where(local == (m + i).astype(jnp.float32), 1.0, 0.0).astype(jnp.bfloat16)
            for i in range(2)
        ]
        top = jnp.concatenate([zt_ref[0:side, :] * mask for mask in masks], axis=0)
        low = jnp.concatenate([zt_ref[side:, :] * mask for mask in masks], axis=0)
        top = lax.dot_general(
            top, upper[...], NN, preferred_element_type=jnp.float32
        ) + lax.dot_general(top, lower[...], NN, preferred_element_type=jnp.float32)
        low = lax.dot_general(low, mixed[...], NN, preferred_element_type=jnp.float32)
        low = low[:, 0:side] + low[:, side:]
        for i in range(2):
            at = slice(i * side, (i + 1) * side)
            gram[m + i, 0:side, :] = top[at] + ridge_member * eye[0:side]
            gram[m + i, side:, 0:side] = jnp.zeros((side, side), jnp.float32)
            gram[m + i, side:, side:] = low[at] + ridge_member * eye[side:, side:]

    member = lax.broadcasted_iota(jnp.int32, (count, slots), 0).astype(jnp.float32)
    masked = jnp.where(member == local, resid_row, 0.0)
    high = masked.astype(jnp.bfloat16)
    low = (masked - high.astype(jnp.float32)).astype(jnp.bfloat16)
    goal = lax.dot_general(
        jnp.concatenate([high, low], axis=0), z_ref[...], NN, preferred_element_type=jnp.float32
    )
    goal = goal[0:count] + goal[count:]

    place = lax.broadcasted_iota(jnp.int32, (1, width), 1)
    turn = lax.broadcasted_iota(jnp.int32, (count, width), 0)
    lane = lax.broadcasted_iota(jnp.int32, (BLOCK, LANES), 1)
    unit = lax.broadcasted_iota(jnp.int32, (BLOCK, width), 1)
    unit = unit - lax.broadcasted_iota(jnp.int32, (BLOCK, width), 0)
    later = []

    def trailing(m, first, inside, left, right):
        update = lax.dot_general(left, right, TN, preferred_element_type=jnp.float32)
        gram[m, first:width, :] = jnp.where(inside, 0.0, gram[m, first:width, :]) - update

    rows_now = [gram[m, 0:BLOCK, :] for m in range(count)]
    for b in range(blocks):
        lo, hi = b * BLOCK, (b + 1) * BLOCK
        packed = [
            jnp.concatenate([rows_now[m][:, lo:hi] for m in range(at, at + per)], axis=1)
            for at in range(0, count, per)
        ]
        for step, packed in enumerate(invert_blocks(packed)):
            if later and step % 2 == 1:
                later.pop(0)()
        while later:
            later.pop(0)()
        inside = (place >= lo) & (place < hi)
        panels = []
        for index, value in enumerate(packed):
            left = jnp.concatenate(
                [jnp.where(lane // BLOCK == i, value, 0.0) for i in range(per)], axis=0
            )
            right = jnp.concatenate(
                [
                    jnp.where(inside, jnp.where(unit == lo, -1.0, 0.0), rows_now[index * per + i])
                    for i in range(per)
                ],
                axis=0,
            )
            got = lax.dot_general(
                split_six(left, 1, True), split_six(right, 0, False), NN,
                preferred_element_type=jnp.float32,
            )
            panels += [got[i * BLOCK : (i + 1) * BLOCK, :] for i in range(per)]
        heads = split_six(goal[:, lo:hi], 1, True)
        goal = jnp.where(inside, 0.0, goal)
        following = []
        for m in range(count):
            right = split_six(panels[m], 0, False)
            if hi < width:
                left = split_six(rows_now[m][:, hi:], 0, True)
                update = lax.dot_general(
                    left[:, 0:BLOCK], right, TN, preferred_element_type=jnp.float32
                )
                following.append(jnp.where(inside, 0.0, gram[m, hi : hi + BLOCK, :]) - update)
                if hi + BLOCK < width:
                    later.append(
                        functools.partial(
                            trailing, m, hi + BLOCK, inside, left[:, BLOCK:], right
                        )
                    )
            update = lax.dot_general(heads, right, NN, preferred_element_type=jnp.float32)
            goal = goal - jnp.where(turn == m, update, 0.0)
        rows_now = following
    return -goal


def window_kernel(
    n_grp, n_mem,
    feat_hbm, re_hbm, member_hbm, slot_hbm, label_hbm, offset_hbm, scale_hbm, start_hbm,
    weight_ref, coef_ref, offsets_ref,
    feat, feat_t, re_ref, member_ref, slot_ref, label_ref, offset_ref, scale_ref, vec_w,
    vec_u, vec_r, vec_p, curv, score, along_ref, rest_ref, near_send, near_recv, far_send, far_recv, one_send, one_recv,
    pick, z_send, z_ref, zt_ref, w_send, w_recv, c_recv, gram, upper, lower, mixed, row_vals,
    load_sem, feat_sem, ns_sem, nr_sem, fs_sem, fr_sem, os_sem, or_sem, zs_sem, zr_sem, ws_sem, wr_sem, cs_sem, cr_sem,
):
    rows, width = feat.shape
    lines = width // LANES
    half = lines // PARTS
    slots = z_ref.shape[0]
    cap = slots // n_mem
    each = (n_mem - 1) // (NEWTON * CG_ITERS)
    early = n_mem - each * NEWTON * CG_ITERS
    direct = n_grp * n_mem <= 32
    me_grp = lax.axis_index("grp")
    me_mem = lax.axis_index("mem")

    loads = [
        pltpu.make_async_copy(source, target, load_sem.at[i])
        for i, (source, target) in enumerate(
            (
                (scale_hbm, scale_ref), (start_hbm, vec_w), (offset_hbm, offset_ref),
                (label_hbm, label_ref), (slot_hbm, slot_ref), (member_hbm, member_ref),
                (re_hbm, re_ref),
            )
        )
    ]
    feat_loads = [
        pltpu.make_async_copy(
            feat_hbm.at[pl.ds(first, 256)], feat.at[pl.ds(first, 256)], feat_sem.at[first // 256]
        )
        for first in range(0, rows, 256)
    ]
    for load in loads + feat_loads:
        load.start()

    low = 2
    high = n_mem // low
    near = n_grp * low
    me_low = lax.rem(me_mem, low)
    me_high = me_mem // low
    me_near = me_grp * low + me_low

    def near_peer(turn):
        other = lax.rem(me_near + turn, near)
        return (other // low, me_high * low + lax.rem(other, low))

    def far_peer(turn):
        return (me_grp, lax.rem(me_high + turn, high) * low + me_low)

    me_all = me_grp * n_mem + me_mem

    def any_peer(turn):
        other = lax.rem(me_all + turn, n_grp * n_mem)
        return (other // n_mem, lax.rem(other, n_mem))

    barrier = pltpu.get_barrier_semaphore()
    if direct:
        for turn in range(1, n_grp * n_mem):
            pl.semaphore_signal(barrier, inc=1, device_id=any_peer(turn), device_id_type=MESH_ID)
        greeted = n_grp * n_mem - 1
    else:
        for turn in range(1, n_mem):
            pl.semaphore_signal(
                barrier, inc=1, device_id=(me_grp, lax.rem(me_mem + turn, n_mem)), device_id_type=MESH_ID
            )
        for turn in range(1, near):
            pl.semaphore_signal(barrier, inc=1, device_id=near_peer(turn), device_id_type=MESH_ID)
        greeted = n_mem - 1 + near - 1

    def peer(turn):
        return (me_grp, lax.rem(me_mem + turn, n_mem))

    def z_copy(turn):
        return pltpu.make_async_remote_copy(
            src_ref=z_send.at[turn - 1],
            dst_ref=z_ref.at[pl.ds(pl.multiple_of((turn - 1) * cap, cap), cap)],
            send_sem=zs_sem.at[turn - 1],
            recv_sem=zr_sem.at[turn - 1],
            device_id=peer(turn),
            device_id_type=MESH_ID,
        )

    def build(turn):
        first = pl.multiple_of(lax.rem(me_mem + turn, n_mem) * cap, cap)
        at = lax.broadcasted_iota(jnp.int32, (cap, rows), 0) + first
        chosen = jnp.where(at == slot_ref[...], 1.0, 0.0).astype(jnp.bfloat16)
        pick[pl.ds(first, cap), :] = chosen
        block = lax.dot_general(chosen, re_ref[...], NN, preferred_element_type=jnp.float32)
        block = block.astype(jnp.bfloat16)

        @pl.when(turn < n_mem)
        def _():
            z_send[turn - 1] = block

        @pl.when(turn == n_mem)
        def _():
            z_ref[(n_mem - 1) * cap :, :] = block

    def begin(value, call, part, size, me, peer_of, source, slots_of, sends, recvs):
        at = pl.ds(part * half, half)
        source[call, at] = value
        for turn in range(1, size):
            pltpu.make_async_remote_copy(
                src_ref=source.at[call, at],
                dst_ref=slots_of.at[call, me, at],
                send_sem=sends.at[call, part],
                recv_sem=recvs.at[call, part],
                device_id=peer_of(turn),
                device_id_type=MESH_ID,
            ).start()
        slots_of[call, me, at] = value

    def finish(call, part, size, slots_of, sends, recvs):
        at = pl.ds(part * half, half)
        others = slots_of.at[call, pl.ds(0, size - 1), at]
        pltpu.make_async_copy(others, others, recvs.at[call, part]).wait()
        pltpu.make_async_copy(others, others, sends.at[call, part]).wait()
        return tree_sum([slots_of[call, i, at] for i in range(size)])

    def begin_near(value, call, part):
        begin(value, call, part, near, me_near, near_peer, near_send, near_recv, ns_sem, nr_sem)

    def finish_near(call, part):
        return finish(call, part, near, near_recv, ns_sem, nr_sem)

    def begin_far(value, call, part):
        begin(value, call, part, high, me_high, far_peer, far_send, far_recv, fs_sem, fr_sem)

    def finish_far(call, part):
        return finish(call, part, high, far_recv, fs_sem, fr_sem)

    def turn_of(place):
        if n_mem != len(ORDER):
            return place + 1
        if isinstance(place, int):
            return ORDER[place]
        turn = jnp.int32(ORDER[0])
        for i, value in enumerate(ORDER):
            turn = jnp.where(place == i, jnp.int32(value), turn)
        return turn

    def regroup(call):
        for q in range(each):
            build(turn_of(early + call * each + q))

    def forward(call):
        for q in range(each):
            turn = turn_of(early + call * each + q)

            @pl.when(turn < n_mem)
            def _():
                z_copy(turn).start()

    def settle(turn):
        @pl.when(turn < n_mem)
        def _():
            z_copy(turn).wait()

        if cap % LANES == 0:
            at = pl.ds(pl.multiple_of((turn - 1) * cap, cap), cap)
            zt_ref[:, at] = z_ref[at, :].T

    def turn_over(call):
        for q in range(each):
            settle(turn_of(call * each + q))

        @pl.when(call == NEWTON * CG_ITERS - 1)
        def _():
            for q in range(early):
                settle(turn_of((call + 1) * each + q))

    def reduce_columns(row, call):
        pair = pair_rows(row)
        for part in range(PARTS):
            begin_near(times_columns(pair, part), call, part)
        @pl.when(call == 0)
        def _():
            transpose_features()

        regroup(call)
        for part in range(PARTS):
            begin_far(finish_near(call, part), call, part)
        turn_over(call)
        sums, image = [], None
        for part in range(PARTS):
            value = scale[part * half : (part + 1) * half] * finish_far(call, part)
            if part == PARTS - 1:
                forward(call)
            got = times_rows(value, part)
            image = got if image is None else image + got
            sums.append(value)
        return jnp.concatenate(sums, axis=0), image

    def small_sum(value, call, between):
        if direct:
            value = jnp.broadcast_to(value, (1, LANES))
            one_send[call] = value
            for turn in range(1, n_grp * n_mem):
                pltpu.make_async_remote_copy(
                    src_ref=one_send.at[call],
                    dst_ref=one_recv.at[call, me_all],
                    send_sem=os_sem.at[call],
                    recv_sem=or_sem.at[call],
                    device_id=any_peer(turn),
                    device_id_type=MESH_ID,
                ).start()
            one_recv[call, me_all] = value
            between()
            others = one_recv.at[call, pl.ds(0, n_grp * n_mem - 1)]
            pltpu.make_async_copy(others, others, or_sem.at[call]).wait()
            pltpu.make_async_copy(others, others, os_sem.at[call]).wait()
            return tree_sum([one_recv[call, i] for i in range(n_grp * n_mem)])[:, 0:1]
        between()
        call = NEWTON * CG_ITERS + call
        begin_near(jnp.broadcast_to(value, (half, LANES)), call, 0)
        begin_far(finish_near(call, 0), call, 0)
        return finish_far(call, 0)[0:1, 0:1]

    def first_rows(vector):
        pair = pair_rows(jnp.concatenate([vector[i : i + 1, :] for i in range(lines)], axis=1))
        parts = []
        for first in range(0, rows, 256):
            feat_loads[first // 256].wait()
            got = lax.dot_general(
                pair, feat[first : first + 256, :], NT, preferred_element_type=jnp.float32
            )
            parts.append(got[0:1] + got[1:2] + got[2:3])
        return jnp.concatenate(parts, axis=1)

    def transpose_features():
        @pl.loop(0, rows // 256)
        def _(r):
            at = pl.ds(pl.multiple_of(r * 256, 256), 256)
            for first in range(0, width, 256):
                feat_t[first : first + 256, at] = feat[at, first : first + 256].T

    def times_rows(value, part):
        vector = scale[part * half : (part + 1) * half] * value
        pair = pair_rows(jnp.concatenate([vector[i : i + 1, :] for i in range(half)], axis=1))
        at = slice(part * half * LANES, (part + 1) * half * LANES)
        parts = []
        for first in range(0, rows, 256):
            got = lax.dot_general(
                pair, feat_t[at, first : first + 256], NN, preferred_element_type=jnp.float32
            )
            parts.append(got[0:1] + got[1:2] + got[2:3])
        return jnp.concatenate(parts, axis=1)

    def times_columns(pair, part):
        parts = []
        for first in range(part * half * LANES, (part + 1) * half * LANES, 256):
            got = lax.dot_general(
                pair, feat[:, first : first + 256], NN, preferred_element_type=jnp.float32
            )
            got = got[0:1] + got[1:2] + got[2:3]
            parts += [got[:, at : at + LANES] for at in range(0, 256, LANES)]
        return jnp.concatenate(parts, axis=0)

    def total(value):
        return jnp.sum(jnp.sum(value, axis=1, keepdims=True), axis=0, keepdims=True)

    for load in loads:
        load.wait()
    scale = scale_ref[...]
    target = label_ref[...].astype(jnp.float32)

    for place in range(early):
        build(turn_of(place))
    pl.semaphore_wait(barrier, greeted)
    for place in range(early):
        z_copy(turn_of(place)).start()
    score[...] = first_rows(scale * vec_w[...])

    def newton(step, carry):
        weights = vec_w[...]
        margin = score[...] + offset_ref[...]
        prob = 1.0 / (1.0 + jnp.exp(-margin))
        curv[...] = prob * (1.0 - prob)

        base = step * CG_ITERS
        summed, along = reduce_columns(prob - target, base)
        resid = -(summed + ridge_fixed * weights)
        along = -(along + ridge_fixed * score[...])
        vec_r[...] = resid
        vec_p[...] = resid
        vec_u[...] = jnp.zeros_like(resid)
        rest_ref[...] = along
        along_ref[...] = along

        def cg(k, norm):
            direction = vec_p[...]
            along = along_ref[...]
            image, seen = reduce_columns(curv[...] * along, base + 1 + k)
            image = image + ridge_fixed * direction
            size = norm / total(direction * image)
            vec_u[...] = vec_u[...] + size * direction
            score[...] = score[...] + size * along
            left = vec_r[...] - size * image
            vec_r[...] = left
            rest = rest_ref[...] - size * (seen + ridge_fixed * along)
            rest_ref[...] = rest
            new_norm = total(left * left)
            turned = new_norm / norm
            vec_p[...] = left + turned * direction
            along_ref[...] = rest + turned * along
            return new_norm

        norm = lax.fori_loop(0, CG_ITERS - 1, cg, total(resid * resid))
        direction = vec_p[...]
        along = along_ref[...]

        def hand_out():
            @pl.when(step == NEWTON - 1)
            def _():
                send_rows(along)

        bend = small_sum(total(curv[...] * along * along), step, hand_out)
        size = norm / (bend + ridge_fixed * total(direction * direction))
        score[...] = score[...] + size * along
        vec_w[...] = weights + (vec_u[...] + size * direction)
        return size

    def send_rows(along):
        row_vals[...] = jnp.zeros_like(row_vals)
        row_vals[0:1, :] = score[...]
        row_vals[1:2, :] = along
        row_vals[2:3, :] = target
        row_vals[3:4, :] = lax.rem(member_ref[...], MEM_DEV).astype(jnp.float32) + 1.0
        parts = jnp.concatenate([p.astype(jnp.float32) for p in three_parts(row_vals[...])], axis=0)
        parts = jnp.concatenate([parts, jnp.zeros_like(parts[0:8])], axis=0).astype(jnp.bfloat16)
        for turn in range(1, n_mem + 1):
            first = pl.multiple_of(lax.rem(me_mem + turn, n_mem) * cap, cap)
            got = lax.dot_general(
                parts, pick[pl.ds(first, cap), :], NT, preferred_element_type=jnp.float32
            )
            got = got[0:8] + got[8:16] + got[16:24]
            if turn < n_mem:
                w_send[turn - 1] = got
                pltpu.make_async_remote_copy(
                    src_ref=w_send.at[turn - 1],
                    dst_ref=w_recv.at[turn - 1],
                    send_sem=ws_sem,
                    recv_sem=wr_sem,
                    device_id=peer(turn),
                    device_id_type=MESH_ID,
                ).start()
            else:
                w_recv[n_mem - 1] = got

    size = lax.fori_loop(0, NEWTON, newton, jnp.zeros((1, 1), jnp.float32))
    weight_ref[...] = vec_w[...]
    if cap % LANES:
        for first in range(0, slots, LANES):
            zt_ref[:, first : first + LANES] = z_ref[first : first + LANES, :].T
    others = w_recv.at[pl.ds(0, n_mem - 1)]
    pltpu.make_async_copy(others, others, wr_sem).wait()
    pltpu.make_async_copy(w_send, w_send, ws_sem).wait()
    arrived = jnp.concatenate([w_recv[t] for t in range(n_mem)], axis=1)
    prob = 1.0 / (1.0 + jnp.exp(-(arrived[0:1] + size * arrived[1:2])))
    coef = fit_members(
        z_ref, zt_ref, prob * (1.0 - prob), prob - arrived[2:3], arrived[3:4] - 1.0,
        gram, upper, lower, mixed,
    )
    coef_ref[...] = coef
    for turn in range(1, n_mem):
        pltpu.make_async_remote_copy(
            src_ref=coef_ref,
            dst_ref=c_recv.at[me_mem],
            send_sem=cs_sem,
            recv_sem=cr_sem,
            device_id=peer(turn),
            device_id_type=MESH_ID,
        ).start()
    c_recv[me_mem] = coef
    others = c_recv.at[pl.ds(0, n_mem - 1)]
    pltpu.make_async_copy(others, others, cr_sem).wait()
    pltpu.make_async_copy(others, others, cs_sem).wait()
    coefs = jnp.concatenate([c_recv[i] for i in range(n_mem)], axis=0)
    upper_part = coefs.astype(jnp.bfloat16)
    lower_part = (coefs - upper_part.astype(jnp.float32)).astype(jnp.bfloat16)
    got = lax.dot_general(
        jnp.concatenate([upper_part, lower_part], axis=0), re_ref[...], NT,
        preferred_element_type=jnp.float32,
    )
    members = n_mem * MEM_DEV
    at = lax.broadcasted_iota(jnp.int32, (members, rows), 0)
    own = at == lax.rem(member_ref[...], members)
    offsets_ref[...] = jnp.sum(
        jnp.where(own, got[0:members] + got[members:], 0.0), axis=0, keepdims=True
    )


def hand_over(*refs):
    for source, target in zip(refs[:3], refs[3:]):
        target[...] = source[...]


def on_device(n_grp, n_mem, features, re_features, member_id, slot, labels, offsets, feature_scale, w_start):
    rows, width = features.shape
    inner = re_features.shape[1]
    lines = width // LANES
    slots = 2 * rows
    cap = slots // n_mem
    near, high = 2 * n_grp, n_mem // 2
    direct = n_grp * n_mem <= 32
    calls = NEWTON * CG_ITERS if direct else NEWTON * (CG_ITERS + 1)
    every = n_grp * n_mem if direct else 2
    f32, bf16, i32 = jnp.float32, jnp.bfloat16, jnp.int32
    held = pltpu.VMEM((lines, LANES), f32)
    dma = pltpu.SemaphoreType.DMA
    whole = pl.BlockSpec(memory_space=pltpu.VMEM)
    weights, member_coef, row_offsets = pl.pallas_call(
        functools.partial(window_kernel, n_grp, n_mem),
        out_shape=(
            jax.ShapeDtypeStruct((lines, LANES), f32),
            jax.ShapeDtypeStruct((MEM_DEV, inner), f32),
            jax.ShapeDtypeStruct((1, rows), f32),
        ),
        in_specs=[pl.BlockSpec(memory_space=pl.ANY)] * 8,
        out_specs=(whole,) * 3,
        scratch_shapes=[
            pltpu.VMEM((rows, width), bf16),
            pltpu.VMEM((width, rows), bf16),
            pltpu.VMEM((rows, inner), bf16),
            pltpu.VMEM((1, rows), i32),
            pltpu.VMEM((1, rows), i32),
            pltpu.VMEM((1, rows), i32),
            pltpu.VMEM((1, rows), f32),
            held, held, held, held, held,
            pltpu.VMEM((1, rows), f32),
            pltpu.VMEM((1, rows), f32),
            pltpu.VMEM((1, rows), f32),
            pltpu.VMEM((1, rows), f32),
            pltpu.VMEM((calls, lines, LANES), f32),
            pltpu.VMEM((calls, near, lines, LANES), f32),
            pltpu.VMEM((calls, lines, LANES), f32),
            pltpu.VMEM((calls, high, lines, LANES), f32),
            pltpu.VMEM((NEWTON, 1, LANES), f32),
            pltpu.VMEM((NEWTON, every, 1, LANES), f32),
            pltpu.VMEM((slots, rows), bf16),
            pltpu.VMEM((n_mem - 1, cap, inner), bf16),
            pltpu.VMEM((slots, inner), bf16),
            pltpu.VMEM((inner, slots), bf16),
            pltpu.VMEM((n_mem - 1, 8, cap), f32),
            pltpu.VMEM((n_mem, 8, cap), f32),
            pltpu.VMEM((n_mem, MEM_DEV, inner), f32),
            pltpu.VMEM((MEM_DEV, inner, inner), f32),
            pltpu.VMEM((slots, inner), bf16),
            pltpu.VMEM((slots, inner), bf16),
            pltpu.VMEM((slots, inner), bf16),
            pltpu.VMEM((8, rows), f32),
            dma((7,)),
            dma((rows // 256,)),
            dma((calls, PARTS)),
            dma((calls, PARTS)),
            dma((calls, PARTS)),
            dma((calls, PARTS)),
            dma((NEWTON,)),
            dma((NEWTON,)),
            dma((n_mem - 1,)),
            dma((n_mem - 1,)),
            dma, dma, dma, dma,
        ],
        compiler_params=pltpu.CompilerParams(
            collective_id=0, has_side_effects=True, vmem_limit_bytes=60 << 20
        ),
        name="window",
    )(
        features,
        re_features,
        member_id.reshape(1, rows),
        slot.reshape(1, rows),
        labels.reshape(1, rows),
        offsets.reshape(1, rows),
        feature_scale.reshape(lines, LANES),
        w_start.reshape(lines, LANES),
    )
    weights, member_coef, row_offsets = pl.pallas_call(
        hand_over,
        out_shape=tuple(
            jax.ShapeDtypeStruct(x.shape, x.dtype) for x in (weights, member_coef, row_offsets)
        ),
        in_specs=[whole] * 3,
        out_specs=(whole,) * 3,
        name="hand_over",
    )(weights, member_coef, row_offsets)
    return (weights.reshape(-1), member_coef, row_offsets.reshape(-1))


def solution(mesh):
    placed = (
        P(("grp", "mem"), None),
        P(("grp", "mem"), None),
        P(("grp", "mem")),
        P(("grp", "mem")),
        P(("grp", "mem")),
        P(("grp", "mem")),
        P(),
        P(),
    )
    return jax.shard_map(
        functools.partial(on_device, mesh.shape["grp"], mesh.shape["mem"]),
        mesh=mesh,
        in_specs=placed,
        out_specs=(P(), P(("grp", "mem"), None), P(("grp", "mem"))),
        check_vma=False,
    )
```

```python
import functools

import jax
import jax.numpy as jnp
from jax import lax
from jax.experimental import pallas as pl
from jax.experimental.pallas import tpu as pltpu
from jax.sharding import PartitionSpec as P

MEM_DEV = 8
NEWTON = 2
CG_ITERS = 3
LANES = 128
BLOCK = 32
PARTS = 2
ORDER = (4, 3, 5, 2, 7, 6, 1, 8)

ridge_fixed = 1.0
ridge_member = 1.0
MESH_ID = pl.DeviceIdType.MESH
NT = (((1,), (1,)), ((), ()))
NN = (((1,), (0,)), ((), ()))
TN = (((0,), (0,)), ((), ()))


def three_parts(value):
    first = value.astype(jnp.bfloat16)
    rest = value - first.astype(jnp.float32)
    second = rest.astype(jnp.bfloat16)
    third = (rest - second.astype(jnp.float32)).astype(jnp.bfloat16)
    return first, second, third


def pair_rows(row):
    at = lax.broadcasted_iota(jnp.int32, (16, row.shape[1]), 0)
    both = jnp.zeros((16, row.shape[1]), jnp.float32)
    for i, part in enumerate(three_parts(row)):
        both = jnp.where(at == i, part.astype(jnp.float32), both)
    return both.astype(jnp.bfloat16)


def tree_sum(parts):
    while len(parts) > 1:
        parts = [parts[i] + parts[i + 1] for i in range(0, len(parts), 2)]
    return parts[0]


def split_six(value, axis, left):
    first, second, third = three_parts(value)
    if left:
        return jnp.concatenate([first, first, second, second, first, third], axis=axis)
    return jnp.concatenate([first, second, first, second, third, first], axis=axis)


def invert_blocks(blocks):
    lane = lax.broadcasted_iota(jnp.int32, (BLOCK, LANES), 1)
    sub = lax.broadcasted_iota(jnp.int32, (BLOCK, LANES), 0)
    base = lane // BLOCK * BLOCK
    place = lane % BLOCK

    def column(value, k):
        return jnp.take_along_axis(value, base + k, axis=1)

    def spread(value, k):
        return jnp.broadcast_to(value[k : k + 1, :], (8, LANES))

    def tall(value):
        return jnp.concatenate([value] * (BLOCK // 8), axis=0)

    def start(value):
        left, right = column(value, 0), column(value, 1)
        corner = [spread(col, k) for k in (0, 1) for col in (left, right)]
        return value, left, right, corner

    blocks = [start(value) for value in blocks]
    for k in range(0, BLOCK, 2):
        one, two = place == k, place == k + 1
        at_one, at_two = one[0:8, :], two[0:8, :]
        more = k + 2 < BLOCK
        new = []
        for value, left, right, (a, b, c, d) in blocks:
            ahead = [column(value, k + 2), column(value, k + 3)] if more else []
            inverse = 1.0 / (a * d - b * c)
            a, b, c, d = d * inverse, -b * inverse, -c * inverse, a * inverse

            def update(value, first, second):
                first, second = tall(first), tall(second)
                value = value - left * first - right * second
                return jnp.where(sub == k, first, jnp.where(sub == k + 1, second, value))

            firsts = [a * spread(col, k) + b * spread(col, k + 1) for col in ahead]
            seconds = [c * spread(col, k) + d * spread(col, k + 1) for col in ahead]
            corner = [
                spread(col, at) - spread(left, at) * first - spread(right, at) * second
                for at in ((k + 2, k + 3) if more else ())
                for col, first, second in zip(ahead, firsts, seconds)
            ]
            following = [
                update(col, first, second) for col, first, second in zip(ahead, firsts, seconds)
            ]
            top, low = spread(value, k), spread(value, k + 1)
            first = jnp.where(at_one, a, jnp.where(at_two, b, a * top + b * low))
            second = jnp.where(at_one, c, jnp.where(at_two, d, c * top + d * low))
            value = update(jnp.where(one | two, 0.0, value), first, second)
            new.append((value, *(following or (left, right)), corner or (a, b, c, d)))
        blocks = new
        yield [value for value, *_ in blocks]


def fit_members(z_ref, zt_ref, curv_row, resid_row, local, gram, upper, lower, mixed):
    width = z_ref.shape[1]
    slots = z_ref.shape[0]
    count = MEM_DEV
    per = LANES // BLOCK
    blocks = width // BLOCK
    side = width // 2
    column = jnp.broadcast_to(curv_row, (LANES, slots)).T
    column = jnp.concatenate([column] * (width // LANES), axis=1)
    weighted = z_ref[...].astype(jnp.float32) * column
    first = weighted.astype(jnp.bfloat16)
    second = (weighted - first.astype(jnp.float32)).astype(jnp.bfloat16)
    upper[...] = first
    lower[...] = second
    mixed[:, 0:side] = first[:, side:]
    mixed[:, side:] = second[:, side:]
    eye = (
        lax.broadcasted_iota(jnp.int32, (width, width), 0)
        == lax.broadcasted_iota(jnp.int32, (width, width), 1)
    ).astype(jnp.float32)

    @pl.loop(0, count, step=2)
    def _(m):
        masks = [
            jnp.where(local == (m + i).astype(jnp.float32), 1.0, 0.0).astype(jnp.bfloat16)
            for i in range(2)
        ]
        top = jnp.concatenate([zt_ref[0:side, :] * mask for mask in masks], axis=0)
        low = jnp.concatenate([zt_ref[side:, :] * mask for mask in masks], axis=0)
        top = lax.dot_general(
            top, upper[...], NN, preferred_element_type=jnp.float32
        ) + lax.dot_general(top, lower[...], NN, preferred_element_type=jnp.float32)
        low = lax.dot_general(low, mixed[...], NN, preferred_element_type=jnp.float32)
        low = low[:, 0:side] + low[:, side:]
        for i in range(2):
            at = slice(i * side, (i + 1) * side)
            gram[m + i, 0:side, :] = top[at] + ridge_member * eye[0:side]
            gram[m + i, side:, 0:side] = jnp.zeros((side, side), jnp.float32)
            gram[m + i, side:, side:] = low[at] + ridge_member * eye[side:, side:]

    member = lax.broadcasted_iota(jnp.int32, (count, slots), 0).astype(jnp.float32)
    masked = jnp.where(member == local, resid_row, 0.0)
    high = masked.astype(jnp.bfloat16)
    low = (masked - high.astype(jnp.float32)).astype(jnp.bfloat16)
    goal = lax.dot_general(
        jnp.concatenate([high, low], axis=0), z_ref[...], NN, preferred_element_type=jnp.float32
    )
    goal = goal[0:count] + goal[count:]

    place = lax.broadcasted_iota(jnp.int32, (1, width), 1)
    turn = lax.broadcasted_iota(jnp.int32, (count, width), 0)
    lane = lax.broadcasted_iota(jnp.int32, (BLOCK, LANES), 1)
    unit = lax.broadcasted_iota(jnp.int32, (BLOCK, width), 1)
    unit = unit - lax.broadcasted_iota(jnp.int32, (BLOCK, width), 0)
    later = []

    def trailing(m, first, inside, left, right):
        update = lax.dot_general(left, right, TN, preferred_element_type=jnp.float32)
        gram[m, first:width, :] = jnp.where(inside, 0.0, gram[m, first:width, :]) - update

    rows_now = [gram[m, 0:BLOCK, :] for m in range(count)]
    for b in range(blocks):
        lo, hi = b * BLOCK, (b + 1) * BLOCK
        packed = [
            jnp.concatenate([rows_now[m][:, lo:hi] for m in range(at, at + per)], axis=1)
            for at in range(0, count, per)
        ]
        for step, packed in enumerate(invert_blocks(packed)):
            if later and step % 2 == 1:
                later.pop(0)()
        while later:
            later.pop(0)()
        inside = (place >= lo) & (place < hi)
        panels = []
        for index, value in enumerate(packed):
            left = jnp.concatenate(
                [jnp.where(lane // BLOCK == i, value, 0.0) for i in range(per)], axis=0
            )
            right = jnp.concatenate(
                [
                    jnp.where(inside, jnp.where(unit == lo, -1.0, 0.0), rows_now[index * per + i])
                    for i in range(per)
                ],
                axis=0,
            )
            got = lax.dot_general(
                split_six(left, 1, True), split_six(right, 0, False), NN,
                preferred_element_type=jnp.float32,
            )
            panels += [got[i * BLOCK : (i + 1) * BLOCK, :] for i in range(per)]
        heads = split_six(goal[:, lo:hi], 1, True).astype(jnp.float32)
        heads = jnp.concatenate([heads, jnp.zeros_like(heads)], axis=0).astype(jnp.bfloat16)
        goal = jnp.where(inside, 0.0, goal)
        following = []
        for m in range(count):
            right = split_six(panels[m], 0, False)
            if hi < width:
                left = split_six(rows_now[m][:, hi:], 0, True)
                update = lax.dot_general(
                    jnp.concatenate([left[:, 0:BLOCK].T, heads], axis=0), right, NN,
                    preferred_element_type=jnp.float32,
                )
                following.append(
                    jnp.where(inside, 0.0, gram[m, hi : hi + BLOCK, :]) - update[0:BLOCK]
                )
                update = update[BLOCK : BLOCK + count]
                if hi + BLOCK < width:
                    later.append(
                        functools.partial(
                            trailing, m, hi + BLOCK, inside, left[:, BLOCK:], right
                        )
                    )
            else:
                update = lax.dot_general(heads, right, NN, preferred_element_type=jnp.float32)
                update = update[0:count]
            goal = goal - jnp.where(turn == m, update, 0.0)
        rows_now = following
    return -goal


def window_kernel(
    n_grp, n_mem,
    feat_hbm, re_hbm, member_hbm, slot_hbm, label_hbm, offset_hbm, scale_hbm, start_hbm,
    weight_ref, coef_ref, offsets_ref,
    feat, feat_t, re_ref, member_ref, slot_ref, label_ref, offset_ref, scale_ref, vec_w,
    vec_u, vec_r, vec_p, curv, score, along_ref, rest_ref, near_send, near_recv, far_send, far_recv, one_send, one_recv,
    pick, z_send, z_ref, zt_ref, w_send, w_recv, c_recv, gram, upper, lower, mixed, row_vals,
    load_sem, feat_sem, ns_sem, nr_sem, fs_sem, fr_sem, os_sem, or_sem, zs_sem, zr_sem, ws_sem, wr_sem, cs_sem, cr_sem,
):
    rows, width = feat.shape
    lines = width // LANES
    half = lines // PARTS
    slots = z_ref.shape[0]
    cap = slots // n_mem
    each = (n_mem - 1) // (NEWTON * CG_ITERS)
    early = n_mem - each * NEWTON * CG_ITERS
    direct = n_grp * n_mem <= 32
    me_grp = lax.axis_index("grp")
    me_mem = lax.axis_index("mem")

    loads = [
        pltpu.make_async_copy(source, target, load_sem.at[i])
        for i, (source, target) in enumerate(
            (
                (scale_hbm, scale_ref), (start_hbm, vec_w), (offset_hbm, offset_ref),
                (label_hbm, label_ref), (slot_hbm, slot_ref), (member_hbm, member_ref),
                (re_hbm, re_ref),
            )
        )
    ]
    feat_loads = [
        pltpu.make_async_copy(
            feat_hbm.at[pl.ds(first, 256)], feat.at[pl.ds(first, 256)], feat_sem.at[first // 256]
        )
        for first in range(0, rows, 256)
    ]
    for load in loads + feat_loads:
        load.start()

    low = 2
    high = n_mem // low
    near = n_grp * low
    me_low = lax.rem(me_mem, low)
    me_high = me_mem // low
    me_near = me_grp * low + me_low

    def near_peer(turn):
        other = lax.rem(me_near + turn, near)
        return (other // low, me_high * low + lax.rem(other, low))

    def far_peer(turn):
        return (me_grp, lax.rem(me_high + turn, high) * low + me_low)

    me_all = me_grp * n_mem + me_mem

    def any_peer(turn):
        other = lax.rem(me_all + turn, n_grp * n_mem)
        return (other // n_mem, lax.rem(other, n_mem))

    barrier = pltpu.get_barrier_semaphore()
    if direct:
        for turn in range(1, n_grp * n_mem):
            pl.semaphore_signal(barrier, inc=1, device_id=any_peer(turn), device_id_type=MESH_ID)
        greeted = n_grp * n_mem - 1
    else:
        for turn in range(1, n_mem):
            pl.semaphore_signal(
                barrier, inc=1, device_id=(me_grp, lax.rem(me_mem + turn, n_mem)), device_id_type=MESH_ID
            )
        for turn in range(1, near):
            pl.semaphore_signal(barrier, inc=1, device_id=near_peer(turn), device_id_type=MESH_ID)
        greeted = n_mem - 1 + near - 1

    def peer(turn):
        return (me_grp, lax.rem(me_mem + turn, n_mem))

    def z_copy(turn):
        return pltpu.make_async_remote_copy(
            src_ref=z_send.at[turn - 1],
            dst_ref=z_ref.at[pl.ds(pl.multiple_of((turn - 1) * cap, cap), cap)],
            send_sem=zs_sem.at[turn - 1],
            recv_sem=zr_sem.at[turn - 1],
            device_id=peer(turn),
            device_id_type=MESH_ID,
        )

    def build(turn):
        first = pl.multiple_of(lax.rem(me_mem + turn, n_mem) * cap, cap)
        at = lax.broadcasted_iota(jnp.int32, (cap, rows), 0) + first
        chosen = jnp.where(at == slot_ref[...], 1.0, 0.0).astype(jnp.bfloat16)
        pick[pl.ds(first, cap), :] = chosen
        block = lax.dot_general(chosen, re_ref[...], NN, preferred_element_type=jnp.float32)
        block = block.astype(jnp.bfloat16)

        @pl.when(turn < n_mem)
        def _():
            z_send[turn - 1] = block

        @pl.when(turn == n_mem)
        def _():
            z_ref[(n_mem - 1) * cap :, :] = block

    def begin(value, call, part, size, me, peer_of, source, slots_of, sends, recvs):
        at = pl.ds(part * half, half)
        source[call, at] = value
        for turn in range(1, size):
            pltpu.make_async_remote_copy(
                src_ref=source.at[call, at],
                dst_ref=slots_of.at[call, me, at],
                send_sem=sends.at[call, part],
                recv_sem=recvs.at[call, part],
                device_id=peer_of(turn),
                device_id_type=MESH_ID,
            ).start()
        slots_of[call, me, at] = value

    def finish(call, part, size, slots_of, sends, recvs):
        at = pl.ds(part * half, half)
        others = slots_of.at[call, pl.ds(0, size - 1), at]
        pltpu.make_async_copy(others, others, recvs.at[call, part]).wait()
        pltpu.make_async_copy(others, others, sends.at[call, part]).wait()
        return tree_sum([slots_of[call, i, at] for i in range(size)])

    def begin_near(value, call, part):
        begin(value, call, part, near, me_near, near_peer, near_send, near_recv, ns_sem, nr_sem)

    def finish_near(call, part):
        return finish(call, part, near, near_recv, ns_sem, nr_sem)

    def begin_far(value, call, part):
        begin(value, call, part, high, me_high, far_peer, far_send, far_recv, fs_sem, fr_sem)

    def finish_far(call, part):
        return finish(call, part, high, far_recv, fs_sem, fr_sem)

    def turn_of(place):
        if n_mem != len(ORDER):
            return place + 1
        if isinstance(place, int):
            return ORDER[place]
        turn = jnp.int32(ORDER[0])
        for i, value in enumerate(ORDER):
            turn = jnp.where(place == i, jnp.int32(value), turn)
        return turn

    def regroup(call):
        for q in range(each):
            build(turn_of(early + call * each + q))

    def forward(call):
        for q in range(each):
            turn = turn_of(early + call * each + q)

            @pl.when(turn < n_mem)
            def _():
                z_copy(turn).start()

    def settle(turn):
        @pl.when(turn < n_mem)
        def _():
            z_copy(turn).wait()

        if cap % LANES == 0:
            at = pl.ds(pl.multiple_of((turn - 1) * cap, cap), cap)
            zt_ref[:, at] = z_ref[at, :].T

    def turn_over(call):
        for q in range(each):
            settle(turn_of(call * each + q))

        @pl.when(call == NEWTON * CG_ITERS - 1)
        def _():
            for q in range(early):
                settle(turn_of((call + 1) * each + q))

    def reduce_columns(row, call):
        pair = pair_rows(row)
        for part in range(PARTS):
            begin_near(times_columns(pair, part), call, part)
        @pl.when(call == 0)
        def _():
            transpose_features()

        regroup(call)
        for part in range(PARTS):
            begin_far(finish_near(call, part), call, part)
        forward(call)
        turn_over(call)
        sums, image = [], None
        for part in range(PARTS):
            value = scale[part * half : (part + 1) * half] * finish_far(call, part)
            got = times_rows(value, part)
            image = got if image is None else image + got
            sums.append(value)
        return jnp.concatenate(sums, axis=0), image

    def small_sum(value, call, between):
        if direct:
            value = jnp.broadcast_to(value, (1, LANES))
            one_send[call] = value
            for turn in range(1, n_grp * n_mem):
                pltpu.make_async_remote_copy(
                    src_ref=one_send.at[call],
                    dst_ref=one_recv.at[call, me_all],
                    send_sem=os_sem.at[call],
                    recv_sem=or_sem.at[call],
                    device_id=any_peer(turn),
                    device_id_type=MESH_ID,
                ).start()
            one_recv[call, me_all] = value
            between()
            others = one_recv.at[call, pl.ds(0, n_grp * n_mem - 1)]
            pltpu.make_async_copy(others, others, or_sem.at[call]).wait()
            pltpu.make_async_copy(others, others, os_sem.at[call]).wait()
            return tree_sum([one_recv[call, i] for i in range(n_grp * n_mem)])[:, 0:1]
        between()
        call = NEWTON * CG_ITERS + call
        begin_near(jnp.broadcast_to(value, (half, LANES)), call, 0)
        begin_far(finish_near(call, 0), call, 0)
        return finish_far(call, 0)[0:1, 0:1]

    def first_rows(vector):
        pair = pair_rows(jnp.concatenate([vector[i : i + 1, :] for i in range(lines)], axis=1))
        parts = []
        for first in range(0, rows, 256):
            feat_loads[first // 256].wait()
            got = lax.dot_general(
                pair, feat[first : first + 256, :], NT, preferred_element_type=jnp.float32
            )
            parts.append(got[0:1] + got[1:2] + got[2:3])
        return jnp.concatenate(parts, axis=1)

    def transpose_features():
        @pl.loop(0, rows // 256)
        def _(r):
            at = pl.ds(pl.multiple_of(r * 256, 256), 256)
            for first in range(0, width, 256):
                feat_t[first : first + 256, at] = feat[at, first : first + 256].T

    def times_rows(value, part):
        vector = scale[part * half : (part + 1) * half] * value
        pair = pair_rows(jnp.concatenate([vector[i : i + 1, :] for i in range(half)], axis=1))
        at = slice(part * half * LANES, (part + 1) * half * LANES)
        parts = []
        for first in range(0, rows, 256):
            got = lax.dot_general(
                pair, feat_t[at, first : first + 256], NN, preferred_element_type=jnp.float32
            )
            parts.append(got[0:1] + got[1:2] + got[2:3])
        return jnp.concatenate(parts, axis=1)

    def times_columns(pair, part):
        parts = []
        for first in range(part * half * LANES, (part + 1) * half * LANES, 256):
            got = lax.dot_general(
                pair, feat[:, first : first + 256], NN, preferred_element_type=jnp.float32
            )
            got = got[0:1] + got[1:2] + got[2:3]
            parts += [got[:, at : at + LANES] for at in range(0, 256, LANES)]
        return jnp.concatenate(parts, axis=0)

    def total(value):
        return jnp.sum(jnp.sum(value, axis=1, keepdims=True), axis=0, keepdims=True)

    for load in loads:
        load.wait()
    scale = scale_ref[...]
    target = label_ref[...].astype(jnp.float32)

    for place in range(early):
        build(turn_of(place))
    pl.semaphore_wait(barrier, greeted)
    for place in range(early):
        z_copy(turn_of(place)).start()
    score[...] = first_rows(scale * vec_w[...])

    def newton(step, carry):
        weights = vec_w[...]
        margin = score[...] + offset_ref[...]
        prob = 1.0 / (1.0 + jnp.exp(-margin))
        curv[...] = prob * (1.0 - prob)

        base = step * CG_ITERS
        summed, along = reduce_columns(prob - target, base)
        resid = -(summed + ridge_fixed * weights)
        along = -(along + ridge_fixed * score[...])
        vec_r[...] = resid
        vec_p[...] = resid
        vec_u[...] = jnp.zeros_like(resid)
        rest_ref[...] = along
        along_ref[...] = along

        def cg(k, norm):
            direction = vec_p[...]
            along = along_ref[...]
            image, seen = reduce_columns(curv[...] * along, base + 1 + k)
            image = image + ridge_fixed * direction
            size = norm / total(direction * image)
            vec_u[...] = vec_u[...] + size * direction
            score[...] = score[...] + size * along
            left = vec_r[...] - size * image
            vec_r[...] = left
            rest = rest_ref[...] - size * (seen + ridge_fixed * along)
            rest_ref[...] = rest
            new_norm = total(left * left)
            turned = new_norm / norm
            vec_p[...] = left + turned * direction
            along_ref[...] = rest + turned * along
            return new_norm

        norm = lax.fori_loop(0, CG_ITERS - 1, cg, total(resid * resid))
        direction = vec_p[...]
        along = along_ref[...]

        def hand_out():
            @pl.when(step == NEWTON - 1)
            def _():
                send_rows(along)

        bend = small_sum(total(curv[...] * along * along), step, hand_out)
        size = norm / (bend + ridge_fixed * total(direction * direction))
        score[...] = score[...] + size * along
        vec_w[...] = weights + (vec_u[...] + size * direction)
        return size

    def send_rows(along):
        row_vals[...] = jnp.zeros_like(row_vals)
        row_vals[0:1, :] = score[...]
        row_vals[1:2, :] = along
        row_vals[2:3, :] = target
        row_vals[3:4, :] = lax.rem(member_ref[...], MEM_DEV).astype(jnp.float32) + 1.0
        parts = jnp.concatenate([p.astype(jnp.float32) for p in three_parts(row_vals[...])], axis=0)
        parts = jnp.concatenate([parts, jnp.zeros_like(parts[0:8])], axis=0).astype(jnp.bfloat16)
        for turn in range(1, n_mem + 1):
            first = pl.multiple_of(lax.rem(me_mem + turn, n_mem) * cap, cap)
            got = lax.dot_general(
                parts, pick[pl.ds(first, cap), :], NT, preferred_element_type=jnp.float32
            )
            got = got[0:8] + got[8:16] + got[16:24]
            if turn < n_mem:
                w_send[turn - 1] = got
                pltpu.make_async_remote_copy(
                    src_ref=w_send.at[turn - 1],
                    dst_ref=w_recv.at[turn - 1],
                    send_sem=ws_sem,
                    recv_sem=wr_sem,
                    device_id=peer(turn),
                    device_id_type=MESH_ID,
                ).start()
            else:
                w_recv[n_mem - 1] = got

    size = lax.fori_loop(0, NEWTON, newton, jnp.zeros((1, 1), jnp.float32))
    weight_ref[...] = vec_w[...]
    if cap % LANES:
        for first in range(0, slots, LANES):
            zt_ref[:, first : first + LANES] = z_ref[first : first + LANES, :].T
    others = w_recv.at[pl.ds(0, n_mem - 1)]
    pltpu.make_async_copy(others, others, wr_sem).wait()
    pltpu.make_async_copy(w_send, w_send, ws_sem).wait()
    arrived = jnp.concatenate([w_recv[t] for t in range(n_mem)], axis=1)
    prob = 1.0 / (1.0 + jnp.exp(-(arrived[0:1] + size * arrived[1:2])))
    coef = fit_members(
        z_ref, zt_ref, prob * (1.0 - prob), prob - arrived[2:3], arrived[3:4] - 1.0,
        gram, upper, lower, mixed,
    )
    coef_ref[...] = coef
    for turn in range(1, n_mem):
        pltpu.make_async_remote_copy(
            src_ref=coef_ref,
            dst_ref=c_recv.at[me_mem],
            send_sem=cs_sem,
            recv_sem=cr_sem,
            device_id=peer(turn),
            device_id_type=MESH_ID,
        ).start()
    c_recv[me_mem] = coef
    others = c_recv.at[pl.ds(0, n_mem - 1)]
    pltpu.make_async_copy(others, others, cr_sem).wait()
    pltpu.make_async_copy(others, others, cs_sem).wait()
    coefs = jnp.concatenate([c_recv[i] for i in range(n_mem)], axis=0)
    upper_part = coefs.astype(jnp.bfloat16)
    lower_part = (coefs - upper_part.astype(jnp.float32)).astype(jnp.bfloat16)
    got = lax.dot_general(
        jnp.concatenate([upper_part, lower_part], axis=0), re_ref[...], NT,
        preferred_element_type=jnp.float32,
    )
    members = n_mem * MEM_DEV
    at = lax.broadcasted_iota(jnp.int32, (members, rows), 0)
    own = at == lax.rem(member_ref[...], members)
    offsets_ref[...] = jnp.sum(
        jnp.where(own, got[0:members] + got[members:], 0.0), axis=0, keepdims=True
    )


def hand_over(*refs):
    for source, target in zip(refs[:3], refs[3:]):
        target[...] = source[...]


def on_device(n_grp, n_mem, features, re_features, member_id, slot, labels, offsets, feature_scale, w_start):
    rows, width = features.shape
    inner = re_features.shape[1]
    lines = width // LANES
    slots = 2 * rows
    cap = slots // n_mem
    near, high = 2 * n_grp, n_mem // 2
    direct = n_grp * n_mem <= 32
    calls = NEWTON * CG_ITERS if direct else NEWTON * (CG_ITERS + 1)
    every = n_grp * n_mem if direct else 2
    f32, bf16, i32 = jnp.float32, jnp.bfloat16, jnp.int32
    held = pltpu.VMEM((lines, LANES), f32)
    dma = pltpu.SemaphoreType.DMA
    whole = pl.BlockSpec(memory_space=pltpu.VMEM)
    weights, member_coef, row_offsets = pl.pallas_call(
        functools.partial(window_kernel, n_grp, n_mem),
        out_shape=(
            jax.ShapeDtypeStruct((lines, LANES), f32),
            jax.ShapeDtypeStruct((MEM_DEV, inner), f32),
            jax.ShapeDtypeStruct((1, rows), f32),
        ),
        in_specs=[pl.BlockSpec(memory_space=pl.ANY)] * 8,
        out_specs=(whole,) * 3,
        scratch_shapes=[
            pltpu.VMEM((rows, width), bf16),
            pltpu.VMEM((width, rows), bf16),
            pltpu.VMEM((rows, inner), bf16),
            pltpu.VMEM((1, rows), i32),
            pltpu.VMEM((1, rows), i32),
            pltpu.VMEM((1, rows), i32),
            pltpu.VMEM((1, rows), f32),
            held, held, held, held, held,
            pltpu.VMEM((1, rows), f32),
            pltpu.VMEM((1, rows), f32),
            pltpu.VMEM((1, rows), f32),
            pltpu.VMEM((1, rows), f32),
            pltpu.VMEM((calls, lines, LANES), f32),
            pltpu.VMEM((calls, near, lines, LANES), f32),
            pltpu.VMEM((calls, lines, LANES), f32),
            pltpu.VMEM((calls, high, lines, LANES), f32),
            pltpu.VMEM((NEWTON, 1, LANES), f32),
            pltpu.VMEM((NEWTON, every, 1, LANES), f32),
            pltpu.VMEM((slots, rows), bf16),
            pltpu.VMEM((n_mem - 1, cap, inner), bf16),
            pltpu.VMEM((slots, inner), bf16),
            pltpu.VMEM((inner, slots), bf16),
            pltpu.VMEM((n_mem - 1, 8, cap), f32),
            pltpu.VMEM((n_mem, 8, cap), f32),
            pltpu.VMEM((n_mem, MEM_DEV, inner), f32),
            pltpu.VMEM((MEM_DEV, inner, inner), f32),
            pltpu.VMEM((slots, inner), bf16),
            pltpu.VMEM((slots, inner), bf16),
            pltpu.VMEM((slots, inner), bf16),
            pltpu.VMEM((8, rows), f32),
            dma((7,)),
            dma((rows // 256,)),
            dma((calls, PARTS)),
            dma((calls, PARTS)),
            dma((calls, PARTS)),
            dma((calls, PARTS)),
            dma((NEWTON,)),
            dma((NEWTON,)),
            dma((n_mem - 1,)),
            dma((n_mem - 1,)),
            dma, dma, dma, dma,
        ],
        compiler_params=pltpu.CompilerParams(
            collective_id=0, has_side_effects=True, vmem_limit_bytes=60 << 20
        ),
        name="window",
    )(
        features,
        re_features,
        member_id.reshape(1, rows),
        slot.reshape(1, rows),
        labels.reshape(1, rows),
        offsets.reshape(1, rows),
        feature_scale.reshape(lines, LANES),
        w_start.reshape(lines, LANES),
    )
    weights, member_coef, row_offsets = pl.pallas_call(
        hand_over,
        out_shape=tuple(
            jax.ShapeDtypeStruct(x.shape, x.dtype) for x in (weights, member_coef, row_offsets)
        ),
        in_specs=[whole] * 3,
        out_specs=(whole,) * 3,
        name="hand_over",
    )(weights, member_coef, row_offsets)
    return (weights.reshape(-1), member_coef, row_offsets.reshape(-1))


def solution(mesh):
    placed = (
        P(("grp", "mem"), None),
        P(("grp", "mem"), None),
        P(("grp", "mem")),
        P(("grp", "mem")),
        P(("grp", "mem")),
        P(("grp", "mem")),
        P(),
        P(),
    )
    return jax.shard_map(
        functools.partial(on_device, mesh.shape["grp"], mesh.shape["mem"]),
        mesh=mesh,
        in_specs=placed,
        out_specs=(P(), P(("grp", "mem"), None), P(("grp", "mem"))),
        check_vma=False,
    )
```

```python
import functools

import jax
import jax.numpy as jnp
from jax import lax
from jax.experimental import pallas as pl
from jax.experimental.pallas import tpu as pltpu
from jax.sharding import PartitionSpec as P

MEM_DEV = 8
NEWTON = 2
CG_ITERS = 3
LANES = 128
BLOCK = 32
PARTS = 2
ORDER = (3, 5, 4, 2, 7, 6, 1, 8)

ridge_fixed = 1.0
ridge_member = 1.0
MESH_ID = pl.DeviceIdType.MESH
NT = (((1,), (1,)), ((), ()))
NN = (((1,), (0,)), ((), ()))
TN = (((0,), (0,)), ((), ()))


def three_parts(value):
    first = value.astype(jnp.bfloat16)
    rest = value - first.astype(jnp.float32)
    second = rest.astype(jnp.bfloat16)
    third = (rest - second.astype(jnp.float32)).astype(jnp.bfloat16)
    return first, second, third


def pair_rows(row):
    at = lax.broadcasted_iota(jnp.int32, (16, row.shape[1]), 0)
    both = jnp.zeros((16, row.shape[1]), jnp.float32)
    for i, part in enumerate(three_parts(row)):
        both = jnp.where(at == i, part.astype(jnp.float32), both)
    return both.astype(jnp.bfloat16)


def tree_sum(parts):
    while len(parts) > 1:
        parts = [parts[i] + parts[i + 1] for i in range(0, len(parts), 2)]
    return parts[0]


def split_six(value, axis, left):
    first, second, third = three_parts(value)
    if left:
        return jnp.concatenate([first, first, second, second, first, third], axis=axis)
    return jnp.concatenate([first, second, first, second, third, first], axis=axis)


def invert_blocks(blocks):
    lane = lax.broadcasted_iota(jnp.int32, (BLOCK, LANES), 1)
    sub = lax.broadcasted_iota(jnp.int32, (BLOCK, LANES), 0)
    base = lane // BLOCK * BLOCK
    place = lane % BLOCK

    def column(value, k):
        return jnp.take_along_axis(value, base + k, axis=1)

    def spread(value, k):
        return jnp.broadcast_to(value[k : k + 1, :], (8, LANES))

    def tall(value):
        return jnp.concatenate([value] * (BLOCK // 8), axis=0)

    def start(value):
        left, right = column(value, 0), column(value, 1)
        corner = [spread(col, k) for k in (0, 1) for col in (left, right)]
        return value, left, right, corner

    blocks = [start(value) for value in blocks]
    for k in range(0, BLOCK, 2):
        one, two = place == k, place == k + 1
        at_one, at_two = one[0:8, :], two[0:8, :]
        more = k + 2 < BLOCK
        new = []
        for value, left, right, (a, b, c, d) in blocks:
            ahead = [column(value, k + 2), column(value, k + 3)] if more else []
            inverse = 1.0 / (a * d - b * c)
            a, b, c, d = d * inverse, -b * inverse, -c * inverse, a * inverse

            def update(value, first, second):
                first, second = tall(first), tall(second)
                value = value - left * first - right * second
                return jnp.where(sub == k, first, jnp.where(sub == k + 1, second, value))

            firsts = [a * spread(col, k) + b * spread(col, k + 1) for col in ahead]
            seconds = [c * spread(col, k) + d * spread(col, k + 1) for col in ahead]
            corner = [
                spread(col, at) - spread(left, at) * first - spread(right, at) * second
                for at in ((k + 2, k + 3) if more else ())
                for col, first, second in zip(ahead, firsts, seconds)
            ]
            following = [
                update(col, first, second) for col, first, second in zip(ahead, firsts, seconds)
            ]
            top, low = spread(value, k), spread(value, k + 1)
            first = jnp.where(at_one, a, jnp.where(at_two, b, a * top + b * low))
            second = jnp.where(at_one, c, jnp.where(at_two, d, c * top + d * low))
            value = update(jnp.where(one | two, 0.0, value), first, second)
            new.append((value, *(following or (left, right)), corner or (a, b, c, d)))
        blocks = new
        yield [value for value, *_ in blocks]


def fit_members(z_ref, zt_ref, curv_row, resid_row, local, gram, upper, lower, mixed):
    width = z_ref.shape[1]
    slots = z_ref.shape[0]
    count = MEM_DEV
    per = LANES // BLOCK
    blocks = width // BLOCK
    side = width // 2
    column = jnp.broadcast_to(curv_row, (LANES, slots)).T
    column = jnp.concatenate([column] * (width // LANES), axis=1)
    weighted = z_ref[...].astype(jnp.float32) * column
    first = weighted.astype(jnp.bfloat16)
    second = (weighted - first.astype(jnp.float32)).astype(jnp.bfloat16)
    upper[...] = first
    lower[...] = second
    mixed[:, 0:side] = first[:, side:]
    mixed[:, side:] = second[:, side:]
    eye = (
        lax.broadcasted_iota(jnp.int32, (width, width), 0)
        == lax.broadcasted_iota(jnp.int32, (width, width), 1)
    ).astype(jnp.float32)

    @pl.loop(0, count, step=2)
    def _(m):
        masks = [
            jnp.where(local == (m + i).astype(jnp.float32), 1.0, 0.0).astype(jnp.bfloat16)
            for i in range(2)
        ]
        top = jnp.concatenate([zt_ref[0:side, :] * mask for mask in masks], axis=0)
        low = jnp.concatenate([zt_ref[side:, :] * mask for mask in masks], axis=0)
        top = lax.dot_general(
            top, upper[...], NN, preferred_element_type=jnp.float32
        ) + lax.dot_general(top, lower[...], NN, preferred_element_type=jnp.float32)
        low = lax.dot_general(low, mixed[...], NN, preferred_element_type=jnp.float32)
        low = low[:, 0:side] + low[:, side:]
        for i in range(2):
            at = slice(i * side, (i + 1) * side)
            gram[m + i, 0:side, :] = top[at] + ridge_member * eye[0:side]
            gram[m + i, side:, 0:side] = jnp.zeros((side, side), jnp.float32)
            gram[m + i, side:, side:] = low[at] + ridge_member * eye[side:, side:]

    member = lax.broadcasted_iota(jnp.int32, (count, slots), 0).astype(jnp.float32)
    masked = jnp.where(member == local, resid_row, 0.0)
    high = masked.astype(jnp.bfloat16)
    low = (masked - high.astype(jnp.float32)).astype(jnp.bfloat16)
    goal = lax.dot_general(
        jnp.concatenate([high, low], axis=0), z_ref[...], NN, preferred_element_type=jnp.float32
    )
    goal = goal[0:count] + goal[count:]

    place = lax.broadcasted_iota(jnp.int32, (1, width), 1)
    turn = lax.broadcasted_iota(jnp.int32, (count, width), 0)
    lane = lax.broadcasted_iota(jnp.int32, (BLOCK, LANES), 1)
    unit = lax.broadcasted_iota(jnp.int32, (BLOCK, width), 1)
    unit = unit - lax.broadcasted_iota(jnp.int32, (BLOCK, width), 0)
    later = []

    def trailing(m, first, inside, left, right):
        update = lax.dot_general(left, right, TN, preferred_element_type=jnp.float32)
        gram[m, first:width, :] = jnp.where(inside, 0.0, gram[m, first:width, :]) - update

    rows_now = [gram[m, 0:BLOCK, :] for m in range(count)]
    for b in range(blocks):
        lo, hi = b * BLOCK, (b + 1) * BLOCK
        packed = [
            jnp.concatenate([rows_now[m][:, lo:hi] for m in range(at, at + per)], axis=1)
            for at in range(0, count, per)
        ]
        for step, packed in enumerate(invert_blocks(packed)):
            if later and step % 2 == 1:
                later.pop(0)()
        while later:
            later.pop(0)()
        inside = (place >= lo) & (place < hi)
        panels = []
        for index, value in enumerate(packed):
            left = jnp.concatenate(
                [jnp.where(lane // BLOCK == i, value, 0.0) for i in range(per)], axis=0
            )
            right = jnp.concatenate(
                [
                    jnp.where(inside, jnp.where(unit == lo, -1.0, 0.0), rows_now[index * per + i])
                    for i in range(per)
                ],
                axis=0,
            )
            got = lax.dot_general(
                split_six(left, 1, True), split_six(right, 0, False), NN,
                preferred_element_type=jnp.float32,
            )
            panels += [got[i * BLOCK : (i + 1) * BLOCK, :] for i in range(per)]
        heads = split_six(goal[:, lo:hi], 1, True).astype(jnp.float32)
        heads = jnp.concatenate([heads, jnp.zeros_like(heads)], axis=0).astype(jnp.bfloat16)
        goal = jnp.where(inside, 0.0, goal)
        following = []
        for m in range(count):
            right = split_six(panels[m], 0, False)
            if hi < width:
                left = split_six(rows_now[m][:, hi:], 0, True)
                update = lax.dot_general(
                    jnp.concatenate([left[:, 0:BLOCK].T, heads], axis=0), right, NN,
                    preferred_element_type=jnp.float32,
                )
                following.append(
                    jnp.where(inside, 0.0, gram[m, hi : hi + BLOCK, :]) - update[0:BLOCK]
                )
                update = update[BLOCK : BLOCK + count]
                if hi + BLOCK < width:
                    later.append(
                        functools.partial(
                            trailing, m, hi + BLOCK, inside, left[:, BLOCK:], right
                        )
                    )
            else:
                update = lax.dot_general(heads, right, NN, preferred_element_type=jnp.float32)
                update = update[0:count]
            goal = goal - jnp.where(turn == m, update, 0.0)
        rows_now = following
    return -goal


def window_kernel(
    n_grp, n_mem,
    feat_hbm, re_hbm, member_hbm, slot_hbm, label_hbm, offset_hbm, scale_hbm, start_hbm,
    weight_ref, coef_ref, offsets_ref,
    feat, feat_t, re_ref, member_ref, slot_ref, label_ref, offset_ref, scale_ref, vec_w,
    vec_u, vec_r, vec_p, curv, score, along_ref, rest_ref, near_send, near_recv, far_send, far_recv, one_send, one_recv,
    pick, z_send, z_ref, zt_ref, w_send, w_recv, c_recv, gram, upper, lower, mixed, row_vals,
    load_sem, feat_sem, ns_sem, nr_sem, fs_sem, fr_sem, os_sem, or_sem, zs_sem, zr_sem, ws_sem, wr_sem, cs_sem, cr_sem,
):
    rows, width = feat.shape
    lines = width // LANES
    half = lines // PARTS
    slots = z_ref.shape[0]
    cap = slots // n_mem
    each = (n_mem - 1) // (NEWTON * CG_ITERS)
    early = n_mem - each * NEWTON * CG_ITERS
    direct = n_grp * n_mem <= 32
    me_grp = lax.axis_index("grp")
    me_mem = lax.axis_index("mem")

    loads = [
        pltpu.make_async_copy(source, target, load_sem.at[i])
        for i, (source, target) in enumerate(
            (
                (scale_hbm, scale_ref), (start_hbm, vec_w), (offset_hbm, offset_ref),
                (label_hbm, label_ref), (slot_hbm, slot_ref), (member_hbm, member_ref),
                (re_hbm, re_ref),
            )
        )
    ]
    feat_loads = [
        pltpu.make_async_copy(
            feat_hbm.at[pl.ds(first, 256)], feat.at[pl.ds(first, 256)], feat_sem.at[first // 256]
        )
        for first in range(0, rows, 256)
    ]
    for load in loads + feat_loads:
        load.start()

    low = 2
    high = n_mem // low
    near = n_grp * low
    me_low = lax.rem(me_mem, low)
    me_high = me_mem // low
    me_near = me_grp * low + me_low

    def near_peer(turn):
        other = lax.rem(me_near + turn, near)
        return (other // low, me_high * low + lax.rem(other, low))

    def far_peer(turn):
        return (me_grp, lax.rem(me_high + turn, high) * low + me_low)

    me_all = me_grp * n_mem + me_mem

    def any_peer(turn):
        other = lax.rem(me_all + turn, n_grp * n_mem)
        return (other // n_mem, lax.rem(other, n_mem))

    barrier = pltpu.get_barrier_semaphore()
    if direct:
        for turn in range(1, n_grp * n_mem):
            pl.semaphore_signal(barrier, inc=1, device_id=any_peer(turn), device_id_type=MESH_ID)
        greeted = n_grp * n_mem - 1
    else:
        for turn in range(1, n_mem):
            pl.semaphore_signal(
                barrier, inc=1, device_id=(me_grp, lax.rem(me_mem + turn, n_mem)), device_id_type=MESH_ID
            )
        for turn in range(1, near):
            pl.semaphore_signal(barrier, inc=1, device_id=near_peer(turn), device_id_type=MESH_ID)
        greeted = n_mem - 1 + near - 1

    def peer(turn):
        return (me_grp, lax.rem(me_mem + turn, n_mem))

    def z_copy(turn):
        return pltpu.make_async_remote_copy(
            src_ref=z_send.at[turn - 1],
            dst_ref=z_ref.at[pl.ds(pl.multiple_of((turn - 1) * cap, cap), cap)],
            send_sem=zs_sem.at[turn - 1],
            recv_sem=zr_sem.at[turn - 1],
            device_id=peer(turn),
            device_id_type=MESH_ID,
        )

    def build(turn):
        first = pl.multiple_of(lax.rem(me_mem + turn, n_mem) * cap, cap)
        at = lax.broadcasted_iota(jnp.int32, (cap, rows), 0) + first
        chosen = jnp.where(at == slot_ref[...], 1.0, 0.0).astype(jnp.bfloat16)
        pick[pl.ds(first, cap), :] = chosen
        block = lax.dot_general(chosen, re_ref[...], NN, preferred_element_type=jnp.float32)
        block = block.astype(jnp.bfloat16)

        @pl.when(turn < n_mem)
        def _():
            z_send[turn - 1] = block

        @pl.when(turn == n_mem)
        def _():
            z_ref[(n_mem - 1) * cap :, :] = block

    def begin(value, call, part, size, me, peer_of, source, slots_of, sends, recvs):
        at = pl.ds(part * half, half)
        source[call, at] = value
        for turn in range(1, size):
            pltpu.make_async_remote_copy(
                src_ref=source.at[call, at],
                dst_ref=slots_of.at[call, me, at],
                send_sem=sends.at[call, part],
                recv_sem=recvs.at[call, part],
                device_id=peer_of(turn),
                device_id_type=MESH_ID,
            ).start()
        slots_of[call, me, at] = value

    def finish(call, part, size, slots_of, sends, recvs):
        at = pl.ds(part * half, half)
        others = slots_of.at[call, pl.ds(0, size - 1), at]
        pltpu.make_async_copy(others, others, recvs.at[call, part]).wait()
        pltpu.make_async_copy(others, others, sends.at[call, part]).wait()
        return tree_sum([slots_of[call, i, at] for i in range(size)])

    def begin_near(value, call, part):
        begin(value, call, part, near, me_near, near_peer, near_send, near_recv, ns_sem, nr_sem)

    def finish_near(call, part):
        return finish(call, part, near, near_recv, ns_sem, nr_sem)

    def begin_far(value, call, part):
        begin(value, call, part, high, me_high, far_peer, far_send, far_recv, fs_sem, fr_sem)

    def finish_far(call, part):
        return finish(call, part, high, far_recv, fs_sem, fr_sem)

    def turn_of(place):
        if n_mem != len(ORDER):
            return place + 1
        if isinstance(place, int):
            return ORDER[place]
        turn = jnp.int32(ORDER[0])
        for i, value in enumerate(ORDER):
            turn = jnp.where(place == i, jnp.int32(value), turn)
        return turn

    def regroup(call):
        for q in range(each):
            build(turn_of(early + call * each + q))

    def forward(call):
        for q in range(each):
            turn = turn_of(early + call * each + q)

            @pl.when(turn < n_mem)
            def _():
                z_copy(turn).start()

    def settle(turn):
        @pl.when(turn < n_mem)
        def _():
            z_copy(turn).wait()

        if cap % LANES == 0:
            at = pl.ds(pl.multiple_of((turn - 1) * cap, cap), cap)
            zt_ref[:, at] = z_ref[at, :].T

    def turn_over(call):
        for q in range(each):
            settle(turn_of(call * each + q))

        @pl.when(call == NEWTON * CG_ITERS - 1)
        def _():
            for q in range(early):
                settle(turn_of((call + 1) * each + q))

    def reduce_columns(row, call):
        pair = pair_rows(row)
        for part in range(PARTS):
            begin_near(times_columns(pair, part), call, part)
        @pl.when(call == 0)
        def _():
            transpose_features()

        regroup(call)
        for part in range(PARTS):
            begin_far(finish_near(call, part), call, part)
        forward(call)
        turn_over(call)
        sums, image = [], None
        for part in range(PARTS):
            value = scale[part * half : (part + 1) * half] * finish_far(call, part)
            got = times_rows(value, part)
            image = got if image is None else image + got
            sums.append(value)
        return jnp.concatenate(sums, axis=0), image

    def small_sum(value, call, between):
        if direct:
            value = jnp.broadcast_to(value, (1, LANES))
            one_send[call] = value
            for turn in range(1, n_grp * n_mem):
                pltpu.make_async_remote_copy(
                    src_ref=one_send.at[call],
                    dst_ref=one_recv.at[call, me_all],
                    send_sem=os_sem.at[call],
                    recv_sem=or_sem.at[call],
                    device_id=any_peer(turn),
                    device_id_type=MESH_ID,
                ).start()
            one_recv[call, me_all] = value
            between()
            others = one_recv.at[call, pl.ds(0, n_grp * n_mem - 1)]
            pltpu.make_async_copy(others, others, or_sem.at[call]).wait()
            pltpu.make_async_copy(others, others, os_sem.at[call]).wait()
            return tree_sum([one_recv[call, i] for i in range(n_grp * n_mem)])[:, 0:1]
        between()
        call = NEWTON * CG_ITERS + call
        begin_near(jnp.broadcast_to(value, (half, LANES)), call, 0)
        begin_far(finish_near(call, 0), call, 0)
        return finish_far(call, 0)[0:1, 0:1]

    def first_rows(vector):
        pair = pair_rows(jnp.concatenate([vector[i : i + 1, :] for i in range(lines)], axis=1))
        parts = []
        for first in range(0, rows, 256):
            feat_loads[first // 256].wait()
            got = lax.dot_general(
                pair, feat[first : first + 256, :], NT, preferred_element_type=jnp.float32
            )
            parts.append(got[0:1] + got[1:2] + got[2:3])
        return jnp.concatenate(parts, axis=1)

    def transpose_features():
        @pl.loop(0, rows // 256)
        def _(r):
            at = pl.ds(pl.multiple_of(r * 256, 256), 256)
            for first in range(0, width, 256):
                feat_t[first : first + 256, at] = feat[at, first : first + 256].T

    def times_rows(value, part):
        vector = scale[part * half : (part + 1) * half] * value
        pair = pair_rows(jnp.concatenate([vector[i : i + 1, :] for i in range(half)], axis=1))
        at = slice(part * half * LANES, (part + 1) * half * LANES)
        parts = []
        for first in range(0, rows, 256):
            got = lax.dot_general(
                pair, feat_t[at, first : first + 256], NN, preferred_element_type=jnp.float32
            )
            parts.append(got[0:1] + got[1:2] + got[2:3])
        return jnp.concatenate(parts, axis=1)

    def times_columns(pair, part):
        parts = []
        for first in range(part * half * LANES, (part + 1) * half * LANES, 256):
            got = lax.dot_general(
                pair, feat[:, first : first + 256], NN, preferred_element_type=jnp.float32
            )
            got = got[0:1] + got[1:2] + got[2:3]
            parts += [got[:, at : at + LANES] for at in range(0, 256, LANES)]
        return jnp.concatenate(parts, axis=0)

    def total(value):
        return jnp.sum(jnp.sum(value, axis=1, keepdims=True), axis=0, keepdims=True)

    for load in loads:
        load.wait()
    scale = scale_ref[...]
    target = label_ref[...].astype(jnp.float32)

    for place in range(early):
        build(turn_of(place))
    pl.semaphore_wait(barrier, greeted)
    for place in range(early):
        z_copy(turn_of(place)).start()
    score[...] = first_rows(scale * vec_w[...])

    def newton(step, carry):
        weights = vec_w[...]
        margin = score[...] + offset_ref[...]
        prob = 1.0 / (1.0 + jnp.exp(-margin))
        curv[...] = prob * (1.0 - prob)

        base = step * CG_ITERS
        summed, along = reduce_columns(prob - target, base)
        resid = -(summed + ridge_fixed * weights)
        along = -(along + ridge_fixed * score[...])
        vec_r[...] = resid
        vec_p[...] = resid
        vec_u[...] = jnp.zeros_like(resid)
        rest_ref[...] = along
        along_ref[...] = along

        def cg(k, norm):
            direction = vec_p[...]
            along = along_ref[...]
            image, seen = reduce_columns(curv[...] * along, base + 1 + k)
            image = image + ridge_fixed * direction
            size = norm / total(direction * image)
            vec_u[...] = vec_u[...] + size * direction
            score[...] = score[...] + size * along
            left = vec_r[...] - size * image
            vec_r[...] = left
            rest = rest_ref[...] - size * (seen + ridge_fixed * along)
            rest_ref[...] = rest
            new_norm = total(left * left)
            turned = new_norm / norm
            vec_p[...] = left + turned * direction
            along_ref[...] = rest + turned * along
            return new_norm

        norm = lax.fori_loop(0, CG_ITERS - 1, cg, total(resid * resid))
        direction = vec_p[...]
        along = along_ref[...]

        def hand_out():
            @pl.when(step == NEWTON - 1)
            def _():
                send_rows(along)

        bend = small_sum(total(curv[...] * along * along), step, hand_out)
        size = norm / (bend + ridge_fixed * total(direction * direction))
        score[...] = score[...] + size * along
        vec_w[...] = weights + (vec_u[...] + size * direction)
        return size

    def send_rows(along):
        row_vals[...] = jnp.zeros_like(row_vals)
        row_vals[0:1, :] = score[...]
        row_vals[1:2, :] = along
        row_vals[2:3, :] = target
        row_vals[3:4, :] = lax.rem(member_ref[...], MEM_DEV).astype(jnp.float32) + 1.0
        parts = jnp.concatenate([p.astype(jnp.float32) for p in three_parts(row_vals[...])], axis=0)
        parts = jnp.concatenate([parts, jnp.zeros_like(parts[0:8])], axis=0).astype(jnp.bfloat16)
        for turn in range(1, n_mem + 1):
            first = pl.multiple_of(lax.rem(me_mem + turn, n_mem) * cap, cap)
            got = lax.dot_general(
                parts, pick[pl.ds(first, cap), :], NT, preferred_element_type=jnp.float32
            )
            got = got[0:8] + got[8:16] + got[16:24]
            if turn < n_mem:
                w_send[turn - 1] = got
                pltpu.make_async_remote_copy(
                    src_ref=w_send.at[turn - 1],
                    dst_ref=w_recv.at[turn - 1],
                    send_sem=ws_sem,
                    recv_sem=wr_sem,
                    device_id=peer(turn),
                    device_id_type=MESH_ID,
                ).start()
            else:
                w_recv[n_mem - 1] = got

    size = lax.fori_loop(0, NEWTON, newton, jnp.zeros((1, 1), jnp.float32))
    weight_ref[...] = vec_w[...]
    if cap % LANES:
        for first in range(0, slots, LANES):
            zt_ref[:, first : first + LANES] = z_ref[first : first + LANES, :].T
    others = w_recv.at[pl.ds(0, n_mem - 1)]
    pltpu.make_async_copy(others, others, wr_sem).wait()
    pltpu.make_async_copy(w_send, w_send, ws_sem).wait()
    arrived = jnp.concatenate([w_recv[t] for t in range(n_mem)], axis=1)
    prob = 1.0 / (1.0 + jnp.exp(-(arrived[0:1] + size * arrived[1:2])))
    coef = fit_members(
        z_ref, zt_ref, prob * (1.0 - prob), prob - arrived[2:3], arrived[3:4] - 1.0,
        gram, upper, lower, mixed,
    )
    coef_ref[...] = coef
    for turn in range(1, n_mem):
        pltpu.make_async_remote_copy(
            src_ref=coef_ref,
            dst_ref=c_recv.at[me_mem],
            send_sem=cs_sem,
            recv_sem=cr_sem,
            device_id=peer(turn),
            device_id_type=MESH_ID,
        ).start()
    c_recv[me_mem] = coef
    others = c_recv.at[pl.ds(0, n_mem - 1)]
    pltpu.make_async_copy(others, others, cr_sem).wait()
    pltpu.make_async_copy(others, others, cs_sem).wait()
    coefs = jnp.concatenate([c_recv[i] for i in range(n_mem)], axis=0)
    upper_part = coefs.astype(jnp.bfloat16)
    lower_part = (coefs - upper_part.astype(jnp.float32)).astype(jnp.bfloat16)
    got = lax.dot_general(
        jnp.concatenate([upper_part, lower_part], axis=0), re_ref[...], NT,
        preferred_element_type=jnp.float32,
    )
    members = n_mem * MEM_DEV
    at = lax.broadcasted_iota(jnp.int32, (members, rows), 0)
    own = at == lax.rem(member_ref[...], members)
    offsets_ref[...] = jnp.sum(
        jnp.where(own, got[0:members] + got[members:], 0.0), axis=0, keepdims=True
    )


def hand_over(*refs):
    for source, target in zip(refs[:3], refs[3:]):
        target[...] = source[...]


def on_device(n_grp, n_mem, features, re_features, member_id, slot, labels, offsets, feature_scale, w_start):
    rows, width = features.shape
    inner = re_features.shape[1]
    lines = width // LANES
    slots = 2 * rows
    cap = slots // n_mem
    near, high = 2 * n_grp, n_mem // 2
    direct = n_grp * n_mem <= 32
    calls = NEWTON * CG_ITERS if direct else NEWTON * (CG_ITERS + 1)
    every = n_grp * n_mem if direct else 2
    f32, bf16, i32 = jnp.float32, jnp.bfloat16, jnp.int32
    held = pltpu.VMEM((lines, LANES), f32)
    dma = pltpu.SemaphoreType.DMA
    whole = pl.BlockSpec(memory_space=pltpu.VMEM)
    weights, member_coef, row_offsets = pl.pallas_call(
        functools.partial(window_kernel, n_grp, n_mem),
        out_shape=(
            jax.ShapeDtypeStruct((lines, LANES), f32),
            jax.ShapeDtypeStruct((MEM_DEV, inner), f32),
            jax.ShapeDtypeStruct((1, rows), f32),
        ),
        in_specs=[pl.BlockSpec(memory_space=pl.ANY)] * 8,
        out_specs=(whole,) * 3,
        scratch_shapes=[
            pltpu.VMEM((rows, width), bf16),
            pltpu.VMEM((width, rows), bf16),
            pltpu.VMEM((rows, inner), bf16),
            pltpu.VMEM((1, rows), i32),
            pltpu.VMEM((1, rows), i32),
            pltpu.VMEM((1, rows), i32),
            pltpu.VMEM((1, rows), f32),
            held, held, held, held, held,
            pltpu.VMEM((1, rows), f32),
            pltpu.VMEM((1, rows), f32),
            pltpu.VMEM((1, rows), f32),
            pltpu.VMEM((1, rows), f32),
            pltpu.VMEM((calls, lines, LANES), f32),
            pltpu.VMEM((calls, near, lines, LANES), f32),
            pltpu.VMEM((calls, lines, LANES), f32),
            pltpu.VMEM((calls, high, lines, LANES), f32),
            pltpu.VMEM((NEWTON, 1, LANES), f32),
            pltpu.VMEM((NEWTON, every, 1, LANES), f32),
            pltpu.VMEM((slots, rows), bf16),
            pltpu.VMEM((n_mem - 1, cap, inner), bf16),
            pltpu.VMEM((slots, inner), bf16),
            pltpu.VMEM((inner, slots), bf16),
            pltpu.VMEM((n_mem - 1, 8, cap), f32),
            pltpu.VMEM((n_mem, 8, cap), f32),
            pltpu.VMEM((n_mem, MEM_DEV, inner), f32),
            pltpu.VMEM((MEM_DEV, inner, inner), f32),
            pltpu.VMEM((slots, inner), bf16),
            pltpu.VMEM((slots, inner), bf16),
            pltpu.VMEM((slots, inner), bf16),
            pltpu.VMEM((8, rows), f32),
            dma((7,)),
            dma((rows // 256,)),
            dma((calls, PARTS)),
            dma((calls, PARTS)),
            dma((calls, PARTS)),
            dma((calls, PARTS)),
            dma((NEWTON,)),
            dma((NEWTON,)),
            dma((n_mem - 1,)),
            dma((n_mem - 1,)),
            dma, dma, dma, dma,
        ],
        compiler_params=pltpu.CompilerParams(
            collective_id=0, has_side_effects=True, vmem_limit_bytes=60 << 20
        ),
        name="window",
    )(
        features,
        re_features,
        member_id.reshape(1, rows),
        slot.reshape(1, rows),
        labels.reshape(1, rows),
        offsets.reshape(1, rows),
        feature_scale.reshape(lines, LANES),
        w_start.reshape(lines, LANES),
    )
    weights, member_coef, row_offsets = pl.pallas_call(
        hand_over,
        out_shape=tuple(
            jax.ShapeDtypeStruct(x.shape, x.dtype) for x in (weights, member_coef, row_offsets)
        ),
        in_specs=[whole] * 3,
        out_specs=(whole,) * 3,
        name="hand_over",
    )(weights, member_coef, row_offsets)
    return (weights.reshape(-1), member_coef, row_offsets.reshape(-1))


def solution(mesh):
    placed = (
        P(("grp", "mem"), None),
        P(("grp", "mem"), None),
        P(("grp", "mem")),
        P(("grp", "mem")),
        P(("grp", "mem")),
        P(("grp", "mem")),
        P(),
        P(),
    )
    return jax.shard_map(
        functools.partial(on_device, mesh.shape["grp"], mesh.shape["mem"]),
        mesh=mesh,
        in_specs=placed,
        out_specs=(P(), P(("grp", "mem"), None), P(("grp", "mem"))),
        check_vma=False,
    )
```
